128 devices in a mesh: req: 32 (over x, z, core), ch: 4 (over y).
Axes of the slice: x: 4, y: 4, z: 4, core: 2. Of those that a mesh axis runs over, the one named last changes fastest.
Arguments:
- tokens: bfloat16 [49152, 2560], P('req'), may hold values from -6 to 6
- w_in: bfloat16 [2560, 2560], P(None, 'ch'), may hold values from -0.125 to 0.125
- w_gate: bfloat16 [2560, 2560], P(None, 'ch'), may hold values from -0.125 to 0.125
- gate_a: bfloat16 [20, 128, 128], P('ch'), may hold values from -0.5 to 0.5
- gate_i: bfloat16 [20, 128, 128], P('ch'), may hold values from -0.5 to 0.5
- conv_w: float32 [4, 2560], P(None, 'ch'), may hold values from -3 to 3
- decay_rate: float32 [2560], P('ch'), may hold values from 9.765625e-06 to 0.04
- w_out: bfloat16 [2560, 2560], P('ch'), may hold values from -0.15625 to 0.15625
- cached_state: float32 [2048, 2560], P('req', 'ch'), may hold values from -3 to 3
- cached_inputs: bfloat16 [2048, 3, 2560], P('req', None, 'ch'), may hold values from -6 to 6
- span_lengths: int32 [16], replicated, may hold values from 1 to 2048, 16384 in all
- accepted: int32 [2048], P('req'), may hold values from 1 to 16
- owner: int32 [2048, 1], P('req'), may hold values from 0 to 31; in each aligned block of 64 rows (0 to 63, 64 to 127, ...) at most 4 rows name the same one
Outputs:
- mixed: bfloat16 [49152, 2560], P('req', 'ch')
- owned_state: float32 [32, 128, 2560], P('req', None, 'ch')
- owned_inputs: bfloat16 [32, 128, 3, 2560], P('req', None, None, 'ch')
The draws below stay inside these ranges and needn't reach their ends.
Inputs may be any that keep to these rules, and one draw needn't show every extreme that they name: Among the 64 requests of one block no owner is named more than 4 times, a bound that some block reaches. `span_lengths`: the lengths sum to 16384; the longest is exactly 2048.
All inputs are finite; a program needn't handle non-finite values.
Results may differ from the reference program's by a relative error of at most 0.0095.
Values may be sent and summed in bfloat16 or wider, within the bound.
A program may use at most 128 MiB of HBM per device.

```python
import math
import jax
import jax.numpy as jnp
import numpy as np
from jax import lax

D = 2560
R = 2560
GB = 128
CONV = 4
DRAFT = 16
SPAN_ROWS = 512
REQ_DEV = 64
TOK_DEV = 1536
TOKENS = 49152
REQUESTS = 2048
SPAN_TOKENS = 16384
MAXSPAN = 2048
SPANS = 16
CAP = 4
BLOCKS = 20
N_REQ = 32
N_CH = 4


def with_ends(entries, rng, smallest, largest):
    shape = entries.shape
    place = [jax.random.randint(jax.random.fold_in(rng, axis), (), 0, shape[axis]) for axis in range(len(shape))]
    entries = entries.at[tuple(place)].set(smallest)
    longest = shape.index(max(shape))
    place[longest] = (place[longest] + 1) % shape[longest]
    return entries.at[tuple(place)].set(largest)


def with_spikes(values, rng, source, target, blocks, factor):
    def block_of(dim):
        return (jnp.arange(values.shape[dim]) // (values.shape[dim] // blocks)).reshape((-1,) + (1,) * (values.ndim - 1 - dim))

    near = jax.random.permutation(rng, blocks)[block_of(target)]
    other_side = (block_of(target) + blocks // 2) % blocks
    return jnp.where((block_of(source) == near) | (block_of(source) == other_side), factor * values, values)


def level_of(key, dims, shards, smallest, top_value):
    def one(axis_at, shards_of):
        heights = jax.random.uniform(jax.random.fold_in(jax.random.fold_in(key, 6), axis_at), (shards_of,), jnp.float32, smallest / len(shards), top_value / len(shards))
        return jnp.repeat(jnp.exp(heights), dims[axis_at] // shards_of).reshape((-1,) + (1,) * (len(dims) - axis_at - 1))

    factor_of = one(*shards[0])
    for cut in shards[1:]:
        factor_of = factor_of * one(*cut)
    return factor_of


def profile(amount, total, reach, lean):
    portions = [(1 << 20) // math.isqrt(grade ** lean) + 1 for grade in range(2, amount + 1)]
    surplus, counts = total - reach - (amount - 1), [1] * (amount - 1)
    while surplus > 0:
        free = [i for i in range(amount - 1) if counts[i] < reach]
        mass, left = sum([portions[i] for i in free]), surplus
        for i in free:
            extra = min(reach - counts[i], max(1, left * portions[i] // mass), surplus)
            counts[i] = counts[i] + extra
            surplus = surplus - extra
    return np.array([reach] + counts)


def uneven(own_key, number_of, total, limit, skew):
    if number_of == 2:
        one = jax.random.randint(own_key, (), max(1, total - limit), min(limit, total - 1) + 1)
        return jnp.stack([one, total - one])
    sizes = jnp.asarray(profile(number_of, total, limit, skew), jnp.int32)
    couples = (number_of - 1) // 2
    donor, taker = sizes[1:1 + 2 * couples:2], sizes[2:2 + 2 * couples:2]
    room = jnp.minimum(donor - 1, limit - taker)
    shifted = jax.random.randint(jax.random.fold_in(own_key, 1), (couples,), 0, 1 << 20) % (room + 1)
    sizes = sizes.at[1:1 + 2 * couples:2].set(donor - shifted).at[2:2 + 2 * couples:2].set(taker + shifted)
    return sizes[jax.random.permutation(jax.random.fold_in(own_key, 2), number_of)]


def routed_block(rng, own, number, rows, count, top, reach, skew):
    ranking = jax.random.permutation(rng, count)
    packed, common = shares(count, rows * top, reach, skew, True), shares(count, rows * top, reach, skew, False)
    places = jnp.arange(count)

    def named(sizes, turn):
        used = int((sizes > 0).sum())
        fixed = max(1, used // 4)
        moved = fixed + (places - fixed + turn * (used - fixed)) % max(1, count - fixed)
        return jnp.zeros((count,), jnp.int32).at[ranking[jnp.where(places < fixed, places, moved)]].set(jnp.asarray(sizes, jnp.int32))

    sizes = jnp.where(number % 4 == 0, named(packed, number // 4), named(common, number - number // 4 - 1))
    mixed = jax.random.permutation(jax.random.fold_in(own, 3), count)
    donor, taker = mixed[0:count // 2 * 2:2], mixed[1:count // 2 * 2:2]
    room = jnp.minimum(sizes[donor] - 1, reach - sizes[taker]) // 2
    room = jnp.where((donor == ranking[0]) | (taker == ranking[0]) | (sizes[taker] == 0), 0, jnp.maximum(room, 0))
    moved = jax.random.randint(jax.random.fold_in(own, 4), (count // 2,), 0, 1 << 20) % (room + 1)
    sizes = sizes.at[donor].add(-moved).at[taker].add(moved)
    items = jnp.searchsorted(jnp.cumsum(sizes), jnp.arange(rows * top), side="right").astype(jnp.int32)
    table = items.reshape(top, rows).T
    table = table[jax.random.permutation(jax.random.fold_in(own, 1), rows)]
    turn = jax.random.randint(jax.random.fold_in(own, 2), (rows, 1), 0, top)
    return jnp.take_along_axis(table, (jnp.arange(top)[None, :] + turn) % top, axis=1)


def shares(count, total, reach, slope, full):
    weights = [(1 << 20) // math.isqrt(standing ** slope) + 1 for standing in range(1, count + 1)]
    largest = reach if full else min(reach, max(-(-total // count), total * weights[0] // sum(weights)))
    least = 1 if total - largest >= count - 1 else 0
    holding, rest = [largest] + [least] * (count - 1), total - largest - least * (count - 1)
    while rest > 0:
        movable = [i for i in range(1, count) if holding[i] < largest] or [i for i in range(1, count) if holding[i] < reach]
        pool, budget = sum([weights[i] for i in movable]), rest
        for i in movable:
            extra = min(reach - holding[i], max(1, budget * weights[i] // pool), rest)
            holding[i] = holding[i] + extra
            rest = rest - extra
    return np.array(holding)


def noise(rng, shape, spread, reach, shards=(), kind=jnp.bfloat16):
    factor_of = level_of(rng, shape, shards, -0.22, 0.18) if shards else 1.0
    entries = jax.random.normal(rng, shape, jnp.float32) * spread * factor_of
    return jnp.minimum(jnp.maximum(entries, -reach), reach).astype(kind)


def bell_draw_with(stream_key, shape, spread, bound, cuts, heavy, kind=jnp.bfloat16):
    result = spread * jax.random.normal(stream_key, shape, jnp.float32)
    if cuts:
        result = result * level_of(stream_key, shape, cuts, -0.22, 0.18)
    return jnp.clip(with_spikes(result, jax.random.fold_in(stream_key, 3), *heavy), -bound, bound).astype(kind)


def setup_inputs(seed: int = 0) -> dict:
    splits = jax.random.split(jax.random.key(seed), 14)
    tokens = noise(splits[0], (TOKENS, D), 1.0, 6.0, ((0, 32),))
    w_in = noise(splits[1], (D, R), D ** -0.5, 0.125, ((1, 4),))
    w_gate = noise(splits[2], (D, R), D ** -0.5, 0.125, ((1, 4),))
    gate_a = noise(splits[3], (BLOCKS, GB, GB), GB ** -0.5, 0.5, ((0, 4),))
    gate_i = noise(splits[4], (BLOCKS, GB, GB), GB ** -0.5, 0.5, ((0, 4),))
    conv_w = noise(splits[5], (CONV, R), 0.5, 3.0, ((1, 4),), jnp.float32)
    decay_rate = jnp.clip(jnp.exp(math.log(0.04) - 8.317766 * jax.random.uniform(splits[6], (R,), jnp.float32) ** level_of(splits[6], (R,), ((0, 4),), -0.2, 0.2)), 9.765624781721272e-06, 0.04)
    w_out = bell_draw_with(splits[7], (R, D), R ** -0.5, 0.15625, ((0, 4),), (0, 1, 4, 2.0))
    cached_state = noise(splits[8], (REQUESTS, R), 0.5, 3.0, ((0, 32), (1, 4)), jnp.float32)
    cached_inputs = noise(splits[9], (REQUESTS, CONV - 1, R), 1.0, 6.0, ((0, 32), (2, 4)))
    span_lengths = uneven(splits[10], SPANS, SPAN_TOKENS, MAXSPAN, 2).astype(jnp.int32)
    accepted = with_ends(jax.random.randint(splits[11], (REQUESTS,), 1, DRAFT + 1), jax.random.fold_in(splits[11], 1), 1, DRAFT).astype(jnp.int32)
    owner_keys = jax.random.split(jax.random.fold_in(splits[12], 1), REQUESTS // REQ_DEV)
    owner_turns = jax.random.permutation(jax.random.fold_in(splits[12], 3), REQUESTS // REQ_DEV)
    owner = jax.vmap(lambda own, number: routed_block(jax.random.fold_in(splits[12], 2), own, number, REQ_DEV, N_REQ, 1, CAP, 2))(owner_keys, owner_turns).reshape((REQUESTS, 1))
    return dict(tokens=tokens, w_in=w_in, w_gate=w_gate, gate_a=gate_a, gate_i=gate_i, conv_w=conv_w, decay_rate=decay_rate, w_out=w_out, cached_state=cached_state, cached_inputs=cached_inputs, span_lengths=span_lengths, accepted=accepted, owner=owner)


def gate_pair(conv_out, blocks_a, blocks_i, rates):
    row_count = conv_out.shape[0]
    block_count = blocks_a.shape[0]
    block_width = blocks_a.shape[1]
    lowered = lax.optimization_barrier(conv_out.astype(jnp.bfloat16)).astype(jnp.float32)
    lowered = lowered.reshape(row_count, block_count, block_width)
    rate_gate = jax.nn.sigmoid(jnp.einsum('tbk,bkj->tbj', lowered, blocks_a.astype(jnp.float32)).reshape(row_count, -1))
    input_gate = jax.nn.sigmoid(jnp.einsum('tbk,bkj->tbj', lowered, blocks_i.astype(jnp.float32)).reshape(row_count, -1))
    log_decay = -8.0 * rates[None, :] * rate_gate
    drive = jnp.sqrt(-jnp.expm1(2.0 * log_decay)) * input_gate * conv_out
    return (jnp.exp(log_decay), drive)

def advance(state, item):
    factor, push = item
    state = factor * state + push
    return (state, state)

def reference(tokens, w_in, w_gate, gate_a, gate_i, conv_w, decay_rate, w_out, cached_state, cached_inputs, span_lengths, accepted, owner):
    chans = R // N_CH
    blocks_dev = chans // GB
    history = CONV - 1
    grid = tokens.reshape(N_REQ, TOK_DEV, D)
    span_tokens = grid[:, :SPAN_ROWS].reshape(SPAN_TOKENS, D)
    draft_tokens = grid[:, SPAN_ROWS:].reshape(REQUESTS * DRAFT, D)
    firsts = (jnp.cumsum(span_lengths) - span_lengths).astype(jnp.int32)
    positions = jnp.arange(SPAN_TOKENS, dtype=jnp.int32)
    begins = lax.optimization_barrier(jnp.max(jnp.where(firsts[None, :] <= positions[:, None], firsts[None, :], 0), axis=1))
    since_start = positions - begins
    keep = (since_start > 0).astype(jnp.float32)[:, None]
    total = jnp.zeros((TOKENS, D), jnp.float32)
    state_parts = []
    input_parts = []
    for quarter in range(N_CH):
        columns = slice(quarter * chans, (quarter + 1) * chans)
        blocks = slice(quarter * blocks_dev, (quarter + 1) * blocks_dev)
        rates = decay_rate[columns]
        span_inner = jnp.dot(span_tokens, w_in[:, columns], preferred_element_type=jnp.float32).astype(jnp.bfloat16)
        span_branch = jax.nn.gelu(jnp.dot(span_tokens, w_gate[:, columns], preferred_element_type=jnp.float32))
        padded = jnp.concatenate([jnp.zeros((history, chans), jnp.bfloat16), span_inner], 0).astype(jnp.float32)
        span_conv = jnp.zeros((SPAN_TOKENS, chans), jnp.float32)
        for offset in range(CONV):
            valid = (since_start >= offset).astype(jnp.float32)[:, None]
            span_conv = span_conv + conv_w[offset, columns][None, :] * padded[history - offset:history - offset + SPAN_TOKENS] * valid
        decay, drive = gate_pair(span_conv, gate_a[blocks], gate_i[blocks], rates)
        _, span_hidden = lax.scan(advance, jnp.zeros((chans,), jnp.float32), (decay * keep, drive))
        span_gated = (span_branch * span_hidden).astype(jnp.bfloat16)
        draft_inner = jnp.dot(draft_tokens, w_in[:, columns], preferred_element_type=jnp.float32).astype(jnp.bfloat16)
        draft_inner = draft_inner.reshape(REQUESTS, DRAFT, chans)
        draft_branch = jax.nn.gelu(jnp.dot(draft_tokens, w_gate[:, columns], preferred_element_type=jnp.float32))
        extended = jnp.concatenate([cached_inputs[:, :, columns], draft_inner], 1).astype(jnp.float32)
        draft_conv = jnp.zeros((REQUESTS, DRAFT, chans), jnp.float32)
        for offset in range(CONV):
            draft_conv = draft_conv + conv_w[offset, columns][None, None, :] * extended[:, history - offset:history - offset + DRAFT]
        decay_d, drive_d = gate_pair(draft_conv.reshape(REQUESTS * DRAFT, chans), gate_a[blocks], gate_i[blocks], rates)
        decay_d = decay_d.reshape(REQUESTS, DRAFT, chans).transpose(1, 0, 2)
        drive_d = drive_d.reshape(REQUESTS, DRAFT, chans).transpose(1, 0, 2)
        _, draft_hidden = lax.scan(advance, cached_state[:, columns], (decay_d, drive_d))
        draft_hidden = draft_hidden.transpose(1, 0, 2)
        draft_gated = (draft_branch * draft_hidden.reshape(REQUESTS * DRAFT, chans)).astype(jnp.bfloat16)
        gated = jnp.concatenate([span_gated.reshape(N_REQ, SPAN_ROWS, chans), draft_gated.reshape(N_REQ, REQ_DEV * DRAFT, chans)], 1)
        gated = gated.reshape(TOKENS, chans)
        partial_out = jnp.dot(gated, w_out[columns], preferred_element_type=jnp.float32)
        total = total + lax.optimization_barrier(partial_out.astype(jnp.bfloat16)).astype(jnp.float32)
        pick_index = jnp.broadcast_to((accepted - 1).astype(jnp.int32)[:, None, None], (REQUESTS, 1, chans))
        state_parts.append(jnp.take_along_axis(draft_hidden, pick_index, axis=1)[:, 0])
        rows_index = accepted.astype(jnp.int32)[:, None] + jnp.arange(history, dtype=jnp.int32)[None, :]
        rows_index = jnp.broadcast_to(rows_index[:, :, None], (REQUESTS, history, chans))
        input_parts.append(jnp.take_along_axis(extended, rows_index, axis=1))
    new_state = jnp.concatenate(state_parts, -1)
    new_inputs = jnp.concatenate(input_parts, -1).astype(jnp.bfloat16)
    owners = owner[:, 0].astype(jnp.int32)
    source = jnp.arange(REQUESTS, dtype=jnp.int32) // REQ_DEV
    marks = (owners[:, None] == jnp.arange(N_REQ, dtype=jnp.int32)[None, :]).astype(jnp.int32)
    marks = marks.reshape(N_REQ, REQ_DEV, N_REQ)
    earlier = (jnp.cumsum(marks, axis=1) - marks).reshape(REQUESTS, N_REQ)
    slot_rank = lax.optimization_barrier(jnp.sum(earlier * marks.reshape(REQUESTS, N_REQ), axis=1))
    target = owners * (N_REQ * CAP) + source * CAP + slot_rank
    owned_state = jnp.zeros((N_REQ * N_REQ * CAP, R), jnp.float32).at[target].set(new_state)
    owned_inputs = jnp.zeros((N_REQ * N_REQ * CAP, history, R), jnp.bfloat16).at[target].set(new_inputs)
    mixed = total.astype(jnp.bfloat16)
    return (mixed, owned_state.reshape(N_REQ, N_REQ * CAP, R), owned_inputs.reshape(N_REQ, N_REQ * CAP, history, R))
```

```python
import functools

import jax
import jax.numpy as jnp
from jax import lax
from jax.experimental import pallas as pl
from jax.experimental.pallas import tpu as pltpu
from jax.sharding import PartitionSpec as P

CONV = 4
HIST = CONV - 1
DRAFT = 16
SPAN_ROWS = 512
BLOCK = 128
CHUNK = 128
HALF = CHUNK // 2
GROUP = CHUNK // DRAFT
HALO = 16
BACK = 4
MESH = pl.DeviceIdType.MESH
F32 = jnp.float32
BF16 = jnp.bfloat16
SERIES = (0.99999999, -0.49999941, 0.16665585, -0.04159356, 0.00810764, -0.00105947)


def lanes(b):
    return pl.ds(pl.multiple_of(b * BLOCK, BLOCK), BLOCK)


def rows_of(c, count):
    return pl.ds(pl.multiple_of(c * count, count), count)


def kernel(
    lag,
    n_req,
    n_ch,
    span_ref,
    accepted_ref,
    owner_ref,
    conv_ref,
    rate_ref,
    tokens_hbm,
    w_in_hbm,
    w_gate_hbm,
    gate_a_hbm,
    gate_i_hbm,
    w_out_hbm,
    state_hbm,
    cached_hbm,
    mixed_hbm,
    ostate_hbm,
    oin_hbm,
    w_cat,
    w_out,
    tok_d,
    tok_s,
    gw,
    state,
    cached,
    cached_f,
    proj,
    inner,
    branch,
    hidden,
    kept,
    acc_b,
    inner_s,
    branch_s,
    local,
    decays,
    ends_a,
    ends_h,
    sum_send,
    sum_recv,
    own,
    stash_r,
    stash_l,
    send_r,
    send_l,
    recv_l,
    recv_r,
    send2_r,
    send2_l,
    recv2_l,
    recv2_r,
    a2a_send,
    a2a_recv,
    mout,
    ost,
    oin,
    load_sem,
    tok_sem,
    halo_send_sem,
    halo_recv_sem,
    sum_send_sem,
    sum_recv_sem,
    one_send,
    one_recv,
    two_send,
    two_recv,
    a2a_send_sem,
    a2a_recv_sem,
    out_sem,
    end_sem,
):
    chans = w_in_hbm.shape[1]
    blocks = chans // BLOCK
    requests = accepted_ref.shape[1]
    slots = 2 * requests // n_req
    drafts = requests * DRAFT // CHUNK
    spans = SPAN_ROWS // CHUNK
    me = lax.axis_index("req")
    place = lax.axis_index("ch")
    right = lax.rem(place + 1, n_ch)
    left = lax.rem(place + n_ch - 1, n_ch)
    far = lax.rem(place + 2, n_ch)

    def peer(j):
        return lax.rem(me + j, n_req)

    loads = [
        pltpu.make_async_copy(w_in_hbm, w_cat.at[:, pl.ds(0, chans)], load_sem.at[0]),
        pltpu.make_async_copy(w_gate_hbm, w_cat.at[:, pl.ds(chans, chans)], load_sem.at[1]),
        pltpu.make_async_copy(gate_a_hbm, gw.at[:, :, pl.ds(0, BLOCK)], load_sem.at[2]),
        pltpu.make_async_copy(gate_i_hbm, gw.at[:, :, pl.ds(BLOCK, BLOCK)], load_sem.at[3]),
        pltpu.make_async_copy(state_hbm, state, load_sem.at[4]),
        pltpu.make_async_copy(cached_hbm, cached, load_sem.at[5]),
    ]
    for k, source in enumerate((place, right, far, left)):
        columns = pl.ds(pl.multiple_of(source * chans, BLOCK), chans)
        loads.append(
            pltpu.make_async_copy(
                w_out_hbm.at[:, columns], w_out.at[:, pl.ds(k * chans, chans)], load_sem.at[6 + k]
            )
        )

    def load_tokens(c):
        return pltpu.make_async_copy(
            tokens_hbm.at[pl.ds(pl.multiple_of(SPAN_ROWS + c * CHUNK, CHUNK), CHUNK)],
            tok_d.at[rows_of(c, CHUNK)],
            tok_sem.at[c],
        )

    load_span = pltpu.make_async_copy(
        tokens_hbm.at[pl.ds(0, SPAN_ROWS)], tok_s.at[pl.ds(HALO, SPAN_ROWS)], load_sem.at[10]
    )
    load_tokens(0).start()
    for copy in loads[:6]:
        copy.start()
    for copy in loads[6:]:
        copy.start()

    @pl.loop(1, drafts)
    def _(c):
        load_tokens(c).start()

    load_span.start()

    barrier = pltpu.get_barrier_semaphore()

    @pl.loop(1, n_req)
    def _(j):
        pl.semaphore_signal(barrier, inc=1, device_id={"req": peer(j)}, device_id_type=MESH)

    for side in (left, right):
        pl.semaphore_signal(barrier, inc=1, device_id={"ch": side}, device_id_type=MESH)

    def halo_copy():
        return pltpu.make_async_remote_copy(
            src_ref=tokens_hbm.at[pl.ds(SPAN_ROWS - HALO, HALO)],
            dst_ref=tok_s.at[pl.ds(0, HALO)],
            send_sem=halo_send_sem,
            recv_sem=halo_recv_sem,
            device_id={"req": peer(1)},
            device_id_type=MESH,
        )

    def first_copy(c, side):
        source, target, device = ((send_r, recv_l, right), (send_l, recv_r, left))[side]
        return pltpu.make_async_remote_copy(
            src_ref=source.at[c],
            dst_ref=target.at[c],
            send_sem=one_send.at[c, side],
            recv_sem=one_recv.at[c, side],
            device_id={"ch": device},
            device_id_type=MESH,
        )

    def second_copy(c, side):
        source, target, device = ((send2_r, recv2_l, right), (send2_l, recv2_r, left))[side]
        return pltpu.make_async_remote_copy(
            src_ref=source.at[c],
            dst_ref=target.at[c],
            send_sem=two_send.at[c, side],
            recv_sem=two_recv.at[c, side],
            device_id={"ch": device},
            device_id_type=MESH,
        )

    def a2a_copy(j):
        return pltpu.make_async_remote_copy(
            src_ref=a2a_send.at[peer(j)],
            dst_ref=a2a_recv.at[me],
            send_sem=a2a_send_sem.at[j],
            recv_sem=a2a_recv_sem.at[j],
            device_id={"req": peer(j)},
            device_id_type=MESH,
        )

    def sum_copy(j):
        return pltpu.make_async_remote_copy(
            src_ref=sum_send,
            dst_ref=sum_recv.at[j - 1],
            send_sem=sum_send_sem.at[j - 1],
            recv_sem=sum_recv_sem.at[j - 1],
            device_id={"req": peer(j)},
            device_id_type=MESH,
        )

    def spread_accepted():
        across = lax.broadcasted_iota(jnp.int32, (requests, requests), 1)
        down = lax.broadcasted_iota(jnp.int32, (requests, requests), 0)
        column = jnp.sum(
            jnp.where(across == down, accepted_ref[...], 0), axis=1, keepdims=True
        )
        acc_b[...] = jnp.broadcast_to(column, (requests, BLOCK))

    spread_accepted()

    firsts = [jnp.int32(0)]
    for i in range(span_ref.shape[0] - 1):
        firsts.append(firsts[-1] + span_ref[i])

    def project(tokens, count):
        for n in range(0, 2 * chans, 2 * BLOCK):
            proj[pl.ds(0, count), n : n + 2 * BLOCK] = jnp.dot(
                tokens, w_cat[:, n : n + 2 * BLOCK], preferred_element_type=F32
            )

    def gelu(u):
        return (0.5 * u) * (1.0 + jnp.tanh(u * (0.7978845608028654 + 0.035677408136300125 * (u * u))))

    def gates(conv, b):
        both = jnp.dot(conv.astype(BF16), gw[b], preferred_element_type=F32)
        rate_gate = 0.5 + 0.5 * jnp.tanh(0.5 * both[:, :BLOCK])
        input_gate = 0.5 + 0.5 * jnp.tanh(0.5 * both[:, BLOCK:])
        y = (16.0 * rate_ref[:, lanes(b)]) * rate_gate
        series = SERIES[-1]
        for term in SERIES[-2::-1]:
            series = series * y + term
        z = y * series
        drive = z * lax.rsqrt(jnp.maximum(z, 1e-37)) * input_gate * conv
        return jnp.exp(-0.5 * y), drive

    def spread():
        return jnp.concatenate([hidden[b] for b in range(blocks)], 1)

    def project_out(c, gated):
        def share(k):
            return jnp.dot(
                gated, w_out[:, k * chans : (k + 1) * chans], preferred_element_type=F32
            ).astype(BF16)

        part = share(2)
        send_r[c, pl.ds(0, HALF)] = part[:HALF]
        send_l[c, pl.ds(0, HALF)] = part[HALF:]
        part = share(1)
        stash_r[c] = part[:HALF]
        send_r[c, pl.ds(HALF, HALF)] = part[HALF:]
        first_copy(c, 0).start()
        part = share(3)
        send_l[c, pl.ds(HALF, HALF)] = part[:HALF]
        stash_l[c] = part[HALF:]
        first_copy(c, 1).start()
        own[c] = share(0)

    def pass_on(c):
        first_copy(c, 0).wait_recv()
        send2_r[c] = (recv_l[c, pl.ds(0, HALF)].astype(F32) + stash_r[c].astype(F32)).astype(BF16)
        second_copy(c, 0).start()
        first_copy(c, 1).wait_recv()
        send2_l[c] = (recv_r[c, pl.ds(0, HALF)].astype(F32) + stash_l[c].astype(F32)).astype(BF16)
        second_copy(c, 1).start()

    def out_copy(c):
        shift = jnp.where(c < drafts, SPAN_ROWS + c * CHUNK, (c - drafts) * CHUNK)
        return pltpu.make_async_copy(
            mout.at[rows_of(c, CHUNK)],
            mixed_hbm.at[pl.ds(pl.multiple_of(shift, CHUNK), CHUNK)],
            out_sem.at[c],
        )

    def finish(c):
        second_copy(c, 0).wait_recv()
        second_copy(c, 1).wait_recv()
        upper = own[c, pl.ds(0, HALF)].astype(F32) + recv2_l[c].astype(F32)
        lower = own[c, pl.ds(HALF, HALF)].astype(F32) + recv2_r[c].astype(F32)
        upper = upper + recv_r[c, pl.ds(HALF, HALF)].astype(F32)
        lower = lower + recv_l[c, pl.ds(HALF, HALF)].astype(F32)
        mout[rows_of(2 * c, HALF), :] = upper.astype(BF16)
        mout[rows_of(2 * c + 1, HALF), :] = lower.astype(BF16)
        out_copy(c).start()

    load_tokens(0).wait()
    for copy in loads[:6]:
        copy.wait()
    cached_f[...] = cached[...].astype(F32)

    @pl.loop(0, drafts)
    def _(c):
        @pl.when(c > 0)
        def _():
            load_tokens(c).wait()

        project(tok_d[rows_of(c, CHUNK), :], CHUNK)
        for b in range(blocks):
            inner[b] = proj[pl.ds(0, CHUNK), b * BLOCK : (b + 1) * BLOCK].astype(BF16).astype(F32)
        branch[...] = gelu(proj[pl.ds(0, CHUNK), chans:])
        members = rows_of(c, GROUP)
        accepted = acc_b[members, :]

        @pl.loop(0, blocks)
        def _(b):
            rows = [cached_f[j, members, lanes(b)] for j in range(HIST)]
            rows += [inner[b, pl.ds(t, GROUP, stride=DRAFT), :] for t in range(DRAFT)]
            x = jnp.concatenate(rows, 0)
            conv = 0.0
            for k in range(CONV):
                at = (HIST - k) * GROUP
                conv = conv + conv_ref[k : k + 1, lanes(b)] * x[at : at + CHUNK]
            decay, drive = gates(conv, b)
            h = state[members, lanes(b)]
            picked = [jnp.zeros((GROUP, BLOCK), F32) for _ in range(1 + HIST)]
            for t in range(DRAFT):
                part = slice(t * GROUP, (t + 1) * GROUP)
                h = decay[part] * h + drive[part]
                hidden[b, pl.ds(t, GROUP, stride=DRAFT), :] = h
                chosen = accepted == t + 1
                picked[0] = jnp.where(chosen, h, picked[0])
                for j in range(HIST):
                    picked[1 + j] = jnp.where(chosen, rows[t + 1 + j], picked[1 + j])
            for j in range(1 + HIST):
                kept[pl.ds(pl.multiple_of(j * requests + c * GROUP, GROUP), GROUP), lanes(b)] = picked[j]

        gated = (branch[...] * spread()).astype(BF16)

        @pl.when(c == 0)
        def _():
            for copy in loads[6:]:
                copy.wait()
            pl.semaphore_wait(barrier, n_req - 1 + 2)
            halo_copy().start()

        project_out(c, gated)

        @pl.when(c >= lag)
        def _():
            pass_on(c - lag)

    owner_row = owner_ref[...]
    across = lax.broadcasted_iota(jnp.int32, (requests, requests), 1)
    down = lax.broadcasted_iota(jnp.int32, (requests, requests), 0)
    owner_column = jnp.sum(jnp.where(across == down, owner_row, 0), axis=1, keepdims=True)
    same = jnp.where(owner_column == owner_row, 1, 0)
    rank_row = jnp.sum(jnp.where(down < across, same, 0), axis=0, keepdims=True)
    slot_row = owner_row * slots + rank_row
    kinds = 1 + HIST
    tall = n_req * kinds * slots
    item = lax.broadcasted_iota(jnp.int32, (tall, requests), 0)
    slot_of = (item // (kinds * slots)) * slots + item % slots
    kind_of = (item // slots) % kinds
    hit = jnp.where(slot_of == slot_row, 1.0, 0.0)
    total = jnp.zeros((tall, chans), F32)
    for j in range(kinds):
        pick = jnp.where(kind_of == j, hit, 0.0).astype(BF16)
        total = total + jnp.dot(
            pick,
            kept[pl.ds(j * requests, requests), :].astype(BF16),
            preferred_element_type=F32,
        )
    a2a_send[...] = total.astype(BF16).reshape(n_req, kinds * slots, chans)

    @pl.loop(1, n_req)
    def _(j):
        a2a_copy(j).start()

    local_copy = pltpu.make_async_copy(a2a_send.at[me], a2a_recv.at[me], a2a_send_sem.at[0])
    local_copy.start()

    load_span.wait()
    halo_copy().wait_recv()

    @pl.loop(0, 2 * chans // (2 * BLOCK))
    def _(n):
        at = pl.ds(pl.multiple_of(n * 2 * BLOCK, 2 * BLOCK), 2 * BLOCK)
        proj[:, at] = jnp.dot(tok_s[...], w_cat[:, at], preferred_element_type=F32)

    for b in range(blocks):
        inner_s[b] = proj[:, b * BLOCK : (b + 1) * BLOCK].astype(BF16).astype(F32)
    branch_s[...] = gelu(proj[pl.ds(HALO, SPAN_ROWS), chans:])

    @pl.loop(drafts - lag, drafts)
    def _(c):
        pass_on(c)

    step = lax.broadcasted_iota(jnp.int32, (CHUNK, BLOCK), 0)
    offset = (step % GROUP) * DRAFT + step // GROUP

    @pl.loop(0, spans)
    def _(q):
        position = me * SPAN_ROWS + q * CHUNK + offset
        begin = jnp.zeros((CHUNK, BLOCK), jnp.int32)
        for first in firsts:
            begin = jnp.where(first <= position, first, begin)
        age = position - begin

        @pl.loop(0, blocks)
        def _(b):
            base = HALO - HIST + q * CHUNK
            rows = [
                inner_s[b, pl.ds(base + i, GROUP, stride=DRAFT), :] for i in range(DRAFT + HIST)
            ]
            x = jnp.concatenate(rows, 0)
            conv = conv_ref[0:1, lanes(b)] * x[HIST * GROUP : HIST * GROUP + CHUNK]
            for k in range(1, CONV):
                at = (HIST - k) * GROUP
                conv = conv + jnp.where(age >= k, conv_ref[k : k + 1, lanes(b)] * x[at : at + CHUNK], 0.0)
            decay, drive = gates(conv, b)
            decay = jnp.where(age > 0, decay, 0.0)
            h = jnp.zeros((GROUP, BLOCK), F32)
            a = jnp.ones((GROUP, BLOCK), F32)
            for t in range(DRAFT):
                part = slice(t * GROUP, (t + 1) * GROUP)
                h = decay[part] * h + drive[part]
                a = decay[part] * a
                at = pl.ds(pl.multiple_of(q * CHUNK + t * GROUP, GROUP), GROUP)
                local[at, lanes(b)] = h
                decays[at, lanes(b)] = a
            ends_a[rows_of(q, GROUP), lanes(b)] = a
            ends_h[rows_of(q, GROUP), lanes(b)] = h

    def link(s, carry):
        product, value = carry
        at = pl.ds(s, 1)
        a = ends_a[at, :]
        h = ends_h[at, :]
        ends_a[at, :] = product
        ends_h[at, :] = value
        return (a * product, a * value + h)

    product, value = lax.fori_loop(
        0, spans * GROUP, link, (jnp.ones((1, chans), F32), jnp.zeros((1, chans), F32))
    )
    sum_send[...] = jnp.zeros_like(sum_send)
    sum_send[0:1, :] = product
    sum_send[1:2, :] = value
    for j in range(1, BACK + 1):
        sum_copy(j).start()
    for j in range(1, BACK + 1):
        sum_copy(j).wait_recv()
    entering = sum_recv[BACK - 1, 1:2, :]
    for j in range(BACK - 2, -1, -1):
        entering = sum_recv[j, 0:1, :] * entering + sum_recv[j, 1:2, :]

    @pl.loop(0, spans)
    def _(q):
        carry = ends_h[rows_of(q, GROUP), :] + ends_a[rows_of(q, GROUP), :] * entering
        for t in range(DRAFT):
            at = pl.ds(pl.multiple_of(q * CHUNK + t * GROUP, GROUP), GROUP)
            h = local[at, :] + decays[at, :] * carry
            for b in range(blocks):
                hidden[b, pl.ds(t, GROUP, stride=DRAFT), :] = h[:, b * BLOCK : (b + 1) * BLOCK]
        project_out(drafts + q, (branch_s[rows_of(q, CHUNK), :] * spread()).astype(BF16))

        @pl.when(q >= lag)
        def _():
            pass_on(drafts + q - lag)

    local_copy.wait()

    @pl.loop(1, n_req)
    def _(j):
        a2a_copy(j).wait_recv()

    got = a2a_recv[...]
    ost[...] = got[:, :slots].astype(F32).reshape(n_req * slots, chans)
    for j in range(HIST):
        oin[j] = (
            got[:, (1 + j) * slots : (2 + j) * slots].astype(F32).reshape(n_req * slots, chans).astype(BF16)
        )
    ends = [
        pltpu.make_async_copy(ost, ostate_hbm, end_sem.at[0]),
        pltpu.make_async_copy(oin, oin_hbm, end_sem.at[1]),
    ]
    for copy in ends:
        copy.start()

    @pl.loop(drafts + max(spans - lag, 0), drafts + spans)
    def _(c):
        pass_on(c)

    @pl.loop(0, drafts + spans)
    def _(c):
        finish(c)

    halo_copy().wait_send()
    for j in range(1, BACK + 1):
        sum_copy(j).wait_send()

    @pl.loop(1, n_req)
    def _(j):
        a2a_copy(j).wait_send()

    @pl.loop(0, drafts + spans)
    def _(c):
        for side in range(2):
            first_copy(c, side).wait_send()
            second_copy(c, side).wait_send()
        out_copy(c).wait()

    for copy in ends:
        copy.wait()


def per_device(
    n_req,
    n_ch,
    tokens,
    w_in,
    w_gate,
    gate_a,
    gate_i,
    conv_w,
    decay_rate,
    w_out,
    cached_state,
    cached_inputs,
    span_lengths,
    accepted,
    owner,
):
    rows, width = tokens.shape
    chans = w_in.shape[1]
    blocks = chans // BLOCK
    requests = accepted.shape[0]
    slots = 2 * requests // n_req
    kinds = 1 + HIST
    drafts = requests * DRAFT // CHUNK
    spans = SPAN_ROWS // CHUNK
    chunks = drafts + spans
    lag = min(3, spans)
    vmem, anywhere, smem = (
        pl.BlockSpec(memory_space=pltpu.VMEM),
        pl.BlockSpec(memory_space=pl.ANY),
        pl.BlockSpec(memory_space=pltpu.SMEM),
    )
    dma = pltpu.SemaphoreType.DMA
    mixed, ostate, oin = pl.pallas_call(
        functools.partial(kernel, lag, n_req, n_ch),
        out_shape=(
            jax.ShapeDtypeStruct((rows, chans), BF16),
            jax.ShapeDtypeStruct((n_req * slots, chans), F32),
            jax.ShapeDtypeStruct((HIST, n_req * slots, chans), BF16),
        ),
        in_specs=[smem, vmem, vmem, vmem, vmem] + [anywhere] * 8,
        out_specs=(anywhere, anywhere, anywhere),
        scratch_shapes=[
            pltpu.VMEM((width, 2 * chans), BF16),
            pltpu.VMEM((chans, n_ch * chans), BF16),
            pltpu.VMEM((drafts * CHUNK, width), BF16),
            pltpu.VMEM((HALO + SPAN_ROWS, width), BF16),
            pltpu.VMEM((blocks, BLOCK, 2 * BLOCK), BF16),
            pltpu.VMEM((requests, chans), F32),
            pltpu.VMEM((HIST, requests, chans), BF16),
            pltpu.VMEM((HIST, requests, chans), F32),
            pltpu.VMEM((HALO + SPAN_ROWS, 2 * chans), F32),
            pltpu.VMEM((blocks, CHUNK, BLOCK), F32),
            pltpu.VMEM((CHUNK, chans), F32),
            pltpu.VMEM((blocks, CHUNK, BLOCK), F32),
            pltpu.VMEM((kinds * requests, chans), F32),
            pltpu.VMEM((requests, BLOCK), jnp.int32),
            pltpu.VMEM((blocks, HALO + SPAN_ROWS, BLOCK), F32),
            pltpu.VMEM((SPAN_ROWS, chans), F32),
            pltpu.VMEM((SPAN_ROWS, chans), F32),
            pltpu.VMEM((SPAN_ROWS, chans), F32),
            pltpu.VMEM((spans * GROUP, chans), F32),
            pltpu.VMEM((spans * GROUP, chans), F32),
            pltpu.VMEM((8, chans), F32),
            pltpu.VMEM((BACK, 8, chans), F32),
            pltpu.VMEM((chunks, CHUNK, chans), BF16),
            pltpu.VMEM((chunks, HALF, chans), BF16),
            pltpu.VMEM((chunks, HALF, chans), BF16),
            pltpu.VMEM((chunks, CHUNK, chans), BF16),
            pltpu.VMEM((chunks, CHUNK, chans), BF16),
            pltpu.VMEM((chunks, CHUNK, chans), BF16),
            pltpu.VMEM((chunks, CHUNK, chans), BF16),
            pltpu.VMEM((chunks, HALF, chans), BF16),
            pltpu.VMEM((chunks, HALF, chans), BF16),
            pltpu.VMEM((chunks, HALF, chans), BF16),
            pltpu.VMEM((chunks, HALF, chans), BF16),
            pltpu.VMEM((n_req, kinds * slots, chans), BF16),
            pltpu.VMEM((n_req, kinds * slots, chans), BF16),
            pltpu.VMEM((rows, chans), BF16),
            pltpu.VMEM((n_req * slots, chans), F32),
            pltpu.VMEM((HIST, n_req * slots, chans), BF16),
            dma((11,)),
            dma((drafts,)),
            dma,
            dma,
            dma((BACK,)),
            dma((BACK,)),
            dma((chunks, 2)),
            dma((chunks, 2)),
            dma((chunks, 2)),
            dma((chunks, 2)),
            dma((n_req,)),
            dma((n_req,)),
            dma((chunks,)),
            dma((2,)),
        ],
        compiler_params=pltpu.CompilerParams(
            collective_id=0, has_side_effects=True, vmem_limit_bytes=60 * 1024 * 1024
        ),
        name="griffin",
    )(
        span_lengths,
        accepted.reshape(1, requests),
        owner.reshape(1, requests),
        conv_w,
        decay_rate.reshape(1, chans),
        tokens,
        w_in,
        w_gate,
        gate_a,
        gate_i,
        w_out,
        cached_state,
        jnp.transpose(cached_inputs, (1, 0, 2)),
    )
    return (
        mixed,
        ostate.reshape(1, n_req * slots, chans),
        jnp.transpose(oin, (1, 0, 2)).reshape(1, n_req * slots, HIST, chans),
    )


def solution(mesh):
    return jax.shard_map(
        functools.partial(per_device, mesh.shape["req"], mesh.shape["ch"]),
        mesh=mesh,
        in_specs=(
            P("req", None),
            P(None, "ch"),
            P(None, "ch"),
            P("ch", None, None),
            P("ch", None, None),
            P(None, "ch"),
            P("ch"),
            P("ch", None),
            P("req", "ch"),
            P("req", None, "ch"),
            P(),
            P("req"),
            P("req", None),
        ),
        out_specs=(P("req", "ch"), P("req", None, "ch"), P("req", None, None, "ch")),
        check_vma=False,
    )
```

```python
import functools

import jax
import jax.numpy as jnp
from jax import lax
from jax.experimental import pallas as pl
from jax.experimental.pallas import tpu as pltpu
from jax.sharding import PartitionSpec as P

CONV = 4
HIST = CONV - 1
DRAFT = 16
SPAN_ROWS = 512
BLOCK = 128
WIDE = 256
CHUNK = 128
HALF = CHUNK // 2
GROUP = CHUNK // DRAFT
HALO = 16
BACK = 4
MESH = pl.DeviceIdType.MESH
F32 = jnp.float32
BF16 = jnp.bfloat16
SERIES = (0.99999999, -0.49999941, 0.16665585, -0.04159356, 0.00810764, -0.00105947)


def lanes(b):
    return pl.ds(pl.multiple_of(b * BLOCK, BLOCK), BLOCK)


def rows_of(c, count):
    return pl.ds(pl.multiple_of(c * count, count), count)


def kernel(
    lag,
    n_req,
    n_ch,
    span_ref,
    accepted_ref,
    owner_ref,
    conv_ref,
    rate_ref,
    tokens_hbm,
    w_in_hbm,
    w_gate_hbm,
    gate_a_hbm,
    gate_i_hbm,
    w_out_hbm,
    state_hbm,
    cached_hbm,
    mout,
    ost,
    oin,
    w_cat,
    w_out,
    tok,
    gw,
    state,
    cached,
    cached_f,
    proj,
    inner,
    branch,
    hidden,
    kept,
    acc_b,
    inner_s,
    branch_s,
    local,
    decays,
    ends_a,
    ends_h,
    sum_send,
    sum_recv,
    own,
    stash_r,
    stash_l,
    send_r,
    send_l,
    recv_l,
    recv_r,
    send2_r,
    send2_l,
    recv2_l,
    recv2_r,
    a2a_send,
    a2a_recv,
    rates,
    load_sem,
    w_sem,
    tok_sem,
    halo_send_sem,
    halo_recv_sem,
    sum_send_sem,
    sum_recv_sem,
    one_send,
    one_recv,
    two_send,
    two_recv,
    a2a_send_sem,
    a2a_recv_sem,
):
    chans = w_in_hbm.shape[1]
    blocks = chans // BLOCK
    requests = accepted_ref.shape[1]
    slots = 2 * requests // n_req
    drafts = requests * DRAFT // CHUNK
    spans = SPAN_ROWS // CHUNK
    wides = 2 * chans // WIDE
    me = lax.axis_index("req")
    place = lax.axis_index("ch")
    right = lax.rem(place + 1, n_ch)
    left = lax.rem(place + n_ch - 1, n_ch)
    far = lax.rem(place + 2, n_ch)

    def peer(j):
        return lax.rem(me + j, n_req)

    def load_weights(n):
        pieces = []
        for k, source in enumerate((w_in_hbm, w_gate_hbm)):
            low, high = max(n * WIDE, k * chans), min((n + 1) * WIDE, (k + 1) * chans)
            if low < high:
                pieces.append(
                    pltpu.make_async_copy(
                        source.at[:, pl.ds(low - k * chans, high - low)],
                        w_cat.at[:, pl.ds(low, high - low)],
                        w_sem.at[n, k],
                    )
                )
        return pieces

    small = [
        pltpu.make_async_copy(gate_a_hbm, gw.at[:, :, pl.ds(0, BLOCK)], load_sem.at[0]),
        pltpu.make_async_copy(gate_i_hbm, gw.at[:, :, pl.ds(BLOCK, BLOCK)], load_sem.at[1]),
        pltpu.make_async_copy(state_hbm, state, load_sem.at[2]),
        pltpu.make_async_copy(cached_hbm, cached, load_sem.at[3]),
    ]
    load_out = []
    for k, source in enumerate((far, right, left, place)):
        columns = pl.ds(pl.multiple_of(source * chans, BLOCK), chans)
        load_out.append(
            pltpu.make_async_copy(
                w_out_hbm.at[:, columns], w_out.at[:, pl.ds(k * chans, chans)], load_sem.at[4 + k]
            )
        )

    def load_tokens(i):
        return pltpu.make_async_copy(
            tokens_hbm.at[rows_of(i, CHUNK)],
            tok.at[pl.ds(pl.multiple_of(HALO + i * CHUNK, HALO), CHUNK)],
            tok_sem.at[i],
        )

    def token_rows(i):
        return tok[pl.ds(pl.multiple_of(HALO + i * CHUNK, HALO), CHUNK), :]

    load_tokens(spans).start()
    for n in range(wides):
        for copy in load_weights(n):
            copy.start()
    for copy in small:
        copy.start()

    barrier = pltpu.get_barrier_semaphore()

    @pl.loop(1, n_req)
    def _(j):
        pl.semaphore_signal(barrier, inc=1, device_id={"req": peer(j)}, device_id_type=MESH)

    for side in (left, right):
        pl.semaphore_signal(barrier, inc=1, device_id={"ch": side}, device_id_type=MESH)

    def halo_copy():
        return pltpu.make_async_remote_copy(
            src_ref=tokens_hbm.at[pl.ds(SPAN_ROWS - HALO, HALO)],
            dst_ref=tok.at[pl.ds(0, HALO)],
            send_sem=halo_send_sem,
            recv_sem=halo_recv_sem,
            device_id={"req": peer(1)},
            device_id_type=MESH,
        )

    def first_copy(c, side):
        source, target, device = ((send_r, recv_l, right), (send_l, recv_r, left))[side]
        return pltpu.make_async_remote_copy(
            src_ref=source.at[c],
            dst_ref=target.at[c],
            send_sem=one_send.at[c, side],
            recv_sem=one_recv.at[c, side],
            device_id={"ch": device},
            device_id_type=MESH,
        )

    def second_copy(c, side):
        source, target, device = ((send2_r, recv2_l, right), (send2_l, recv2_r, left))[side]
        return pltpu.make_async_remote_copy(
            src_ref=source.at[c],
            dst_ref=target.at[c],
            send_sem=two_send.at[c, side],
            recv_sem=two_recv.at[c, side],
            device_id={"ch": device},
            device_id_type=MESH,
        )

    def a2a_copy(j):
        return pltpu.make_async_remote_copy(
            src_ref=a2a_send.at[peer(j)],
            dst_ref=a2a_recv.at[me],
            send_sem=a2a_send_sem.at[j],
            recv_sem=a2a_recv_sem.at[j],
            device_id={"req": peer(j)},
            device_id_type=MESH,
        )

    def sum_copy(j):
        return pltpu.make_async_remote_copy(
            src_ref=sum_send,
            dst_ref=sum_recv.at[j - 1],
            send_sem=sum_send_sem.at[j - 1],
            recv_sem=sum_recv_sem.at[j - 1],
            device_id={"req": peer(j)},
            device_id_type=MESH,
        )

    def spread_accepted():
        across = lax.broadcasted_iota(jnp.int32, (requests, requests), 1)
        down = lax.broadcasted_iota(jnp.int32, (requests, requests), 0)
        column = jnp.sum(
            jnp.where(across == down, accepted_ref[...], 0), axis=1, keepdims=True
        )
        acc_b[...] = jnp.broadcast_to(column, (requests, BLOCK))

    spread_accepted()

    firsts = [jnp.int32(0)]
    for i in range(span_ref.shape[0] - 1):
        firsts.append(firsts[-1] + span_ref[i])

    def project(tokens, n):
        at = slice(n * WIDE, (n + 1) * WIDE)
        proj[:, at] = jnp.dot(tokens, w_cat[:, at], preferred_element_type=F32)

    def gelu(u):
        return (0.5 * u) * (1.0 + jnp.tanh(u * (0.7978845608028654 + 0.035677408136300125 * (u * u))))

    def gates(conv, b):
        both = jnp.dot(conv.astype(BF16), gw[b], preferred_element_type=F32)
        rate_gate = 0.5 + 0.5 * jnp.tanh(0.5 * both[:, :BLOCK])
        input_gate = 0.5 + 0.5 * jnp.tanh(0.5 * both[:, BLOCK:])
        y = rates[0:1, lanes(b)] * rate_gate
        series = SERIES[-1]
        for term in SERIES[-2::-1]:
            series = series * y + term
        z = y * series
        drive = z * lax.rsqrt(jnp.maximum(z, 1e-37)) * input_gate * conv
        return jnp.exp(-0.5 * y), drive

    def spread():
        return jnp.concatenate([hidden[b] for b in range(blocks)], 1)

    def project_out(c, gated):
        def shares(k):
            at = slice(k * chans, (k + 2) * chans)
            both = jnp.dot(gated, w_out[:, at], preferred_element_type=F32)
            return both[:, :chans].astype(BF16), both[:, chans:].astype(BF16)

        to_far, to_right = shares(0)
        send_r[c, pl.ds(0, HALF)] = to_far[:HALF]
        send_l[c, pl.ds(0, HALF)] = to_far[HALF:]
        stash_r[c] = to_right[:HALF]
        send_r[c, pl.ds(HALF, HALF)] = to_right[HALF:]
        first_copy(c, 0).start()
        to_left, to_own = shares(2)
        send_l[c, pl.ds(HALF, HALF)] = to_left[:HALF]
        stash_l[c] = to_left[HALF:]
        first_copy(c, 1).start()
        own[c] = to_own

    def pass_on(c):
        first_copy(c, 0).wait_recv()
        send2_r[c] = (recv_l[c, pl.ds(0, HALF)].astype(F32) + stash_r[c].astype(F32)).astype(BF16)
        second_copy(c, 0).start()
        first_copy(c, 1).wait_recv()
        send2_l[c] = (recv_r[c, pl.ds(0, HALF)].astype(F32) + stash_l[c].astype(F32)).astype(BF16)
        second_copy(c, 1).start()

    def finish(c):
        second_copy(c, 0).wait_recv()
        second_copy(c, 1).wait_recv()
        upper = own[c, pl.ds(0, HALF)].astype(F32) + recv2_l[c].astype(F32)
        lower = own[c, pl.ds(HALF, HALF)].astype(F32) + recv2_r[c].astype(F32)
        upper = upper + recv_r[c, pl.ds(HALF, HALF)].astype(F32)
        lower = lower + recv_l[c, pl.ds(HALF, HALF)].astype(F32)
        base = jnp.where(c < drafts, SPAN_ROWS + c * CHUNK, (c - drafts) * CHUNK)
        mout[pl.ds(pl.multiple_of(base, HALF), HALF), :] = upper.astype(BF16)
        mout[pl.ds(pl.multiple_of(base + HALF, HALF), HALF), :] = lower.astype(BF16)

    step = lax.broadcasted_iota(jnp.int32, (CHUNK, BLOCK), 0)
    offset = (step % GROUP) * DRAFT + step // GROUP

    def edge_rows():
        halo_copy().wait_recv()
        edge = tok[pl.ds(0, HALO), :]
        for b in range(blocks):
            columns = w_cat[:, b * BLOCK : (b + 1) * BLOCK]
            inner_s[b, pl.ds(0, HALO)] = (
                jnp.dot(edge, columns, preferred_element_type=F32).astype(BF16).astype(F32)
            )

    def span_chunk(q, following):
        for b in range(blocks):
            inner_s[b, pl.ds(pl.multiple_of(HALO + q * CHUNK, HALO), CHUNK)] = (
                proj[:, b * BLOCK : (b + 1) * BLOCK].astype(BF16).astype(F32)
            )
        branch_s[rows_of(q, CHUNK), :] = gelu(proj[:, chans:])
        position = me * SPAN_ROWS + q * CHUNK + offset
        begin = jnp.zeros((CHUNK, BLOCK), jnp.int32)
        for first in firsts:
            begin = jnp.where(first <= position, first, begin)
        age = position - begin
        tokens = token_rows(following)
        base = HALO - HIST + q * CHUNK
        for b in range(blocks):
            project(tokens, b)
            rows = [
                inner_s[b, pl.ds(base + i, GROUP, stride=DRAFT), :] for i in range(DRAFT + HIST)
            ]
            x = jnp.concatenate(rows, 0)
            conv = conv_ref[0:1, lanes(b)] * x[HIST * GROUP : HIST * GROUP + CHUNK]
            for k in range(1, CONV):
                at = (HIST - k) * GROUP
                term = conv_ref[k : k + 1, lanes(b)] * x[at : at + CHUNK]
                conv = conv + jnp.where(age >= k, term, 0.0)
            decay, drive = gates(conv, b)
            decay = jnp.where(age > 0, decay, 0.0)
            h = jnp.zeros((GROUP, BLOCK), F32)
            a = jnp.ones((GROUP, BLOCK), F32)
            for t in range(DRAFT):
                part = slice(t * GROUP, (t + 1) * GROUP)
                h = decay[part] * h + drive[part]
                a = decay[part] * a
                at = pl.ds(pl.multiple_of(q * CHUNK + t * GROUP, GROUP), GROUP)
                local[at, lanes(b)] = h
                decays[at, lanes(b)] = a
            ends_a[rows_of(q, GROUP), lanes(b)] = a
            ends_h[rows_of(q, GROUP), lanes(b)] = h

    def link(s, carry):
        product, value = carry
        at = pl.ds(s, 1)
        a = ends_a[at, :]
        h = ends_h[at, :]
        ends_a[at, :] = product
        ends_h[at, :] = value
        return (a * product, a * value + h)

    def send_sums():
        product, value = lax.fori_loop(
            0, spans * GROUP, link, (jnp.ones((1, chans), F32), jnp.zeros((1, chans), F32))
        )
        sum_send[...] = jnp.zeros_like(sum_send)
        sum_send[0:1, :] = product
        sum_send[1:2, :] = value
        for j in range(1, BACK + 1):
            sum_copy(j).start()

    def draft_chunk(c, following):
        for b in range(blocks):
            inner[b] = proj[:, b * BLOCK : (b + 1) * BLOCK].astype(BF16).astype(F32)
        branch[...] = gelu(proj[:, chans:])
        members = rows_of(c, GROUP)
        accepted = acc_b[members, :]
        chosen = [accepted == t + 1 for t in range(DRAFT)]
        tokens = token_rows(following)
        for b in range(blocks):
            project(tokens, b)
            rows = [cached_f[j, members, lanes(b)] for j in range(HIST)]
            rows += [inner[b, pl.ds(t, GROUP, stride=DRAFT), :] for t in range(DRAFT)]
            x = jnp.concatenate(rows, 0)
            conv = 0.0
            for k in range(CONV):
                at = (HIST - k) * GROUP
                conv = conv + conv_ref[k : k + 1, lanes(b)] * x[at : at + CHUNK]
            decay, drive = gates(conv, b)
            h = state[members, lanes(b)]
            picked = [jnp.zeros((GROUP, BLOCK), F32) for _ in range(1 + HIST)]
            for t in range(DRAFT):
                part = slice(t * GROUP, (t + 1) * GROUP)
                h = decay[part] * h + drive[part]
                hidden[b, pl.ds(t, GROUP, stride=DRAFT), :] = h
                picked[0] = jnp.where(chosen[t], h, picked[0])
                for j in range(HIST):
                    picked[1 + j] = jnp.where(chosen[t], rows[t + 1 + j], picked[1 + j])
            for j in range(1 + HIST):
                at = pl.ds(pl.multiple_of(j * requests + c * GROUP, GROUP), GROUP)
                kept[at, lanes(b)] = picked[j]
        project_out(c, (branch[...] * spread()).astype(BF16))

    load_tokens(spans).wait()
    tokens = token_rows(spans)
    for n in range(wides):
        for copy in load_weights(n):
            copy.wait()
        project(tokens, n)

    for copy in load_out:
        copy.start()
    for q in range(spans):
        load_tokens(q).start()

    @pl.loop(spans + 1, spans + drafts)
    def _(i):
        load_tokens(i).start()

    for copy in small:
        copy.wait()
    cached_f[...] = cached[...].astype(F32)
    rates[0:1, :] = 16.0 * rate_ref[...].reshape(1, chans)
    for copy in load_out:
        copy.wait()
    pl.semaphore_wait(barrier, n_req - 1 + 2)
    halo_copy().start()

    @pl.loop(0, spans)
    def _(i):
        load_tokens(i).wait()
        draft_chunk(i, i)

        @pl.when(i == 0)
        def _():
            edge_rows()

        @pl.when(i >= lag)
        def _():
            pass_on(i - lag)

        load_tokens(spans + 1 + i).wait()
        span_chunk(i, spans + 1 + i)

    send_sums()

    @pl.loop(spans, drafts)
    def _(c):
        @pl.when(c < drafts - 1)
        def _():
            load_tokens(spans + 1 + c).wait()

        draft_chunk(c, spans + jnp.minimum(c + 1, drafts - 1))
        pass_on(c - lag)

    owner_row = owner_ref[...]
    across = lax.broadcasted_iota(jnp.int32, (requests, requests), 1)
    down = lax.broadcasted_iota(jnp.int32, (requests, requests), 0)
    owner_column = jnp.sum(jnp.where(across == down, owner_row, 0), axis=1, keepdims=True)
    same = jnp.where(owner_column == owner_row, 1, 0)
    rank_row = jnp.sum(jnp.where(down < across, same, 0), axis=0, keepdims=True)
    slot_row = owner_row * slots + rank_row
    kinds = 1 + HIST
    tall = n_req * kinds * slots
    item = lax.broadcasted_iota(jnp.int32, (tall, requests), 0)
    slot_of = (item // (kinds * slots)) * slots + item % slots
    kind_of = (item // slots) % kinds
    hit = jnp.where(slot_of == slot_row, 1.0, 0.0)
    total = jnp.zeros((tall, chans), F32)
    for j in range(kinds):
        pick = jnp.where(kind_of == j, hit, 0.0).astype(BF16)
        total = total + jnp.dot(
            pick,
            kept[pl.ds(j * requests, requests), :].astype(BF16),
            preferred_element_type=F32,
        )
    a2a_send[...] = total.astype(BF16).reshape(n_req, kinds * slots, chans)

    @pl.loop(1, n_req)
    def _(j):
        a2a_copy(j).start()

    local_copy = pltpu.make_async_copy(a2a_send.at[me], a2a_recv.at[me], a2a_send_sem.at[0])
    local_copy.start()

    @pl.loop(drafts - lag, drafts)
    def _(c):
        pass_on(c)

    for j in range(1, BACK + 1):
        sum_copy(j).wait_recv()
    entering = sum_recv[BACK - 1, 1:2, :]
    for j in range(BACK - 2, -1, -1):
        entering = sum_recv[j, 0:1, :] * entering + sum_recv[j, 1:2, :]

    @pl.loop(0, spans)
    def _(q):
        carry = ends_h[rows_of(q, GROUP), :] + ends_a[rows_of(q, GROUP), :] * entering
        for t in range(DRAFT):
            at = pl.ds(pl.multiple_of(q * CHUNK + t * GROUP, GROUP), GROUP)
            h = local[at, :] + decays[at, :] * carry
            for b in range(blocks):
                hidden[b, pl.ds(t, GROUP, stride=DRAFT), :] = h[:, b * BLOCK : (b + 1) * BLOCK]
        project_out(drafts + q, (branch_s[rows_of(q, CHUNK), :] * spread()).astype(BF16))

        @pl.when(q >= lag)
        def _():
            pass_on(drafts + q - lag)

    local_copy.wait()

    @pl.loop(1, n_req)
    def _(j):
        a2a_copy(j).wait_recv()

    got = a2a_recv[...]
    ost[...] = got[:, :slots].astype(F32).reshape(n_req * slots, chans)
    for j in range(HIST):
        oin[j] = (
            got[:, (1 + j) * slots : (2 + j) * slots].astype(F32).reshape(n_req * slots, chans).astype(BF16)
        )
    @pl.loop(drafts + max(spans - lag, 0), drafts + spans)
    def _(c):
        pass_on(c)

    @pl.loop(0, drafts + spans)
    def _(c):
        finish(c)

    halo_copy().wait_send()
    for j in range(1, BACK + 1):
        sum_copy(j).wait_send()

    @pl.loop(1, n_req)
    def _(j):
        a2a_copy(j).wait_send()

    @pl.loop(0, drafts + spans)
    def _(c):
        for side in range(2):
            first_copy(c, side).wait_send()
            second_copy(c, side).wait_send()


def per_device(
    n_req,
    n_ch,
    tokens,
    w_in,
    w_gate,
    gate_a,
    gate_i,
    conv_w,
    decay_rate,
    w_out,
    cached_state,
    cached_inputs,
    span_lengths,
    accepted,
    owner,
):
    rows, width = tokens.shape
    chans = w_in.shape[1]
    blocks = chans // BLOCK
    requests = accepted.shape[0]
    slots = 2 * requests // n_req
    kinds = 1 + HIST
    drafts = requests * DRAFT // CHUNK
    spans = SPAN_ROWS // CHUNK
    chunks = drafts + spans
    lag = min(2, spans)
    vmem, anywhere, smem = (
        pl.BlockSpec(memory_space=pltpu.VMEM),
        pl.BlockSpec(memory_space=pl.ANY),
        pl.BlockSpec(memory_space=pltpu.SMEM),
    )
    dma = pltpu.SemaphoreType.DMA
    mixed, ostate, oin = pl.pallas_call(
        functools.partial(kernel, lag, n_req, n_ch),
        out_shape=(
            pltpu.VMEM((rows, chans), BF16),
            pltpu.VMEM((n_req * slots, chans), F32),
            pltpu.VMEM((HIST, n_req * slots, chans), BF16),
        ),
        in_specs=[smem, vmem, vmem, vmem, vmem] + [anywhere] * 8,
        out_specs=(vmem, vmem, vmem),
        scratch_shapes=[
            pltpu.VMEM((width, 2 * chans), BF16),
            pltpu.VMEM((chans, n_ch * chans), BF16),
            pltpu.VMEM((HALO + rows, width), BF16),
            pltpu.VMEM((blocks, BLOCK, 2 * BLOCK), BF16),
            pltpu.VMEM((requests, chans), F32),
            pltpu.VMEM((HIST, requests, chans), BF16),
            pltpu.VMEM((HIST, requests, chans), F32),
            pltpu.VMEM((CHUNK, 2 * chans), F32),
            pltpu.VMEM((blocks, CHUNK, BLOCK), F32),
            pltpu.VMEM((CHUNK, chans), F32),
            pltpu.VMEM((blocks, CHUNK, BLOCK), F32),
            pltpu.VMEM((kinds * requests, chans), F32),
            pltpu.VMEM((requests, BLOCK), jnp.int32),
            pltpu.VMEM((blocks, HALO + SPAN_ROWS, BLOCK), F32),
            pltpu.VMEM((SPAN_ROWS, chans), F32),
            pltpu.VMEM((SPAN_ROWS, chans), F32),
            pltpu.VMEM((SPAN_ROWS, chans), F32),
            pltpu.VMEM((spans * GROUP, chans), F32),
            pltpu.VMEM((spans * GROUP, chans), F32),
            pltpu.VMEM((8, chans), F32),
            pltpu.VMEM((BACK, 8, chans), F32),
            pltpu.VMEM((chunks, CHUNK, chans), BF16),
            pltpu.VMEM((chunks, HALF, chans), BF16),
            pltpu.VMEM((chunks, HALF, chans), BF16),
            pltpu.VMEM((chunks, CHUNK, chans), BF16),
            pltpu.VMEM((chunks, CHUNK, chans), BF16),
            pltpu.VMEM((chunks, CHUNK, chans), BF16),
            pltpu.VMEM((chunks, CHUNK, chans), BF16),
            pltpu.VMEM((chunks, HALF, chans), BF16),
            pltpu.VMEM((chunks, HALF, chans), BF16),
            pltpu.VMEM((chunks, HALF, chans), BF16),
            pltpu.VMEM((chunks, HALF, chans), BF16),
            pltpu.VMEM((n_req, kinds * slots, chans), BF16),
            pltpu.VMEM((n_req, kinds * slots, chans), BF16),
            pltpu.VMEM((8, chans), F32),
            dma((9,)),
            dma((2 * chans // WIDE, 2)),
            dma((chunks,)),
            dma,
            dma,
            dma((BACK,)),
            dma((BACK,)),
            dma((chunks, 2)),
            dma((chunks, 2)),
            dma((chunks, 2)),
            dma((chunks, 2)),
            dma((n_req,)),
            dma((n_req,)),
        ],
        compiler_params=pltpu.CompilerParams(
            collective_id=0, has_side_effects=True, vmem_limit_bytes=52 * 1024 * 1024
        ),
        name="griffin",
    )(
        span_lengths,
        accepted.reshape(1, requests),
        owner.reshape(1, requests),
        conv_w,
        decay_rate,
        tokens,
        w_in,
        w_gate,
        gate_a,
        gate_i,
        w_out,
        cached_state,
        jnp.transpose(cached_inputs, (1, 0, 2)),
    )
    return (
        mixed,
        ostate.reshape(1, n_req * slots, chans),
        jnp.transpose(oin, (1, 0, 2)).reshape(1, n_req * slots, HIST, chans),
    )


def solution(mesh):
    return jax.shard_map(
        functools.partial(per_device, mesh.shape["req"], mesh.shape["ch"]),
        mesh=mesh,
        in_specs=(
            P("req", None),
            P(None, "ch"),
            P(None, "ch"),
            P("ch", None, None),
            P("ch", None, None),
            P(None, "ch"),
            P("ch"),
            P("ch", None),
            P("req", "ch"),
            P("req", None, "ch"),
            P(),
            P("req"),
            P("req", None),
        ),
        out_specs=(P("req", "ch"), P("req", None, "ch"), P("req", None, None, "ch")),
        check_vma=False,
    )
```

```python
import functools

import jax
import jax.numpy as jnp
from jax import lax
from jax.experimental import pallas as pl
from jax.experimental.pallas import tpu as pltpu
from jax.sharding import PartitionSpec as P

CONV = 4
HIST = CONV - 1
DRAFT = 16
SPAN_ROWS = 512
BLOCK = 128
WIDE = 256
CHUNK = 128
HALF = CHUNK // 2
GROUP = CHUNK // DRAFT
HALO = 16
BACK = 4
MESH = pl.DeviceIdType.MESH
F32 = jnp.float32
BF16 = jnp.bfloat16
SERIES = (0.99999999, -0.49999941, 0.16665585, -0.04159356, 0.00810764, -0.00105947)


def lanes(b):
    return pl.ds(pl.multiple_of(b * BLOCK, BLOCK), BLOCK)


def rows_of(c, count):
    return pl.ds(pl.multiple_of(c * count, count), count)


def kernel(
    lag,
    n_req,
    n_ch,
    span_ref,
    accepted_ref,
    owner_ref,
    conv_ref,
    rate_ref,
    tokens_hbm,
    w_in_hbm,
    w_gate_hbm,
    gate_a_hbm,
    gate_i_hbm,
    w_out_hbm,
    state_hbm,
    cached_hbm,
    mout,
    ost,
    oin,
    w_cat,
    w_out,
    tok,
    gw,
    state,
    cached,
    cached_f,
    proj,
    inner,
    branch,
    hidden,
    kept,
    acc_b,
    inner_s,
    branch_s,
    local,
    decays,
    ends_a,
    ends_h,
    sum_send,
    sum_recv,
    own,
    stash_r,
    stash_l,
    send_r,
    send_l,
    recv_l,
    recv_r,
    send2_r,
    send2_l,
    recv2_l,
    recv2_r,
    a2a_send,
    a2a_recv,
    rates,
    load_sem,
    w_sem,
    tok_sem,
    halo_send_sem,
    halo_recv_sem,
    sum_send_sem,
    sum_recv_sem,
    one_send,
    one_recv,
    two_send,
    two_recv,
    a2a_send_sem,
    a2a_recv_sem,
):
    chans = w_in_hbm.shape[1]
    blocks = chans // BLOCK
    requests = accepted_ref.shape[1]
    slots = 2 * requests // n_req
    drafts = requests * DRAFT // CHUNK
    spans = SPAN_ROWS // CHUNK
    wides = 2 * chans // WIDE
    me = lax.axis_index("req")
    place = lax.axis_index("ch")
    right = lax.rem(place + 1, n_ch)
    left = lax.rem(place + n_ch - 1, n_ch)
    far = lax.rem(place + 2, n_ch)

    def peer(j):
        return lax.rem(me + j, n_req)

    def load_weights(n):
        pieces = []
        for k, source in enumerate((w_in_hbm, w_gate_hbm)):
            low, high = max(n * WIDE, k * chans), min((n + 1) * WIDE, (k + 1) * chans)
            if low < high:
                pieces.append(
                    pltpu.make_async_copy(
                        source.at[:, pl.ds(low - k * chans, high - low)],
                        w_cat.at[:, pl.ds(low, high - low)],
                        w_sem.at[n, k],
                    )
                )
        return pieces

    small = [
        pltpu.make_async_copy(gate_a_hbm, gw.at[:, :, pl.ds(0, BLOCK)], load_sem.at[0]),
        pltpu.make_async_copy(gate_i_hbm, gw.at[:, :, pl.ds(BLOCK, BLOCK)], load_sem.at[1]),
        pltpu.make_async_copy(state_hbm, state, load_sem.at[2]),
        pltpu.make_async_copy(cached_hbm, cached, load_sem.at[3]),
    ]
    load_out = []
    for k, source in enumerate((far, right, left, place)):
        columns = pl.ds(pl.multiple_of(source * chans, BLOCK), chans)
        load_out.append(
            pltpu.make_async_copy(
                w_out_hbm.at[:, columns], w_out.at[:, pl.ds(k * chans, chans)], load_sem.at[4 + k]
            )
        )

    def load_tokens(i):
        return pltpu.make_async_copy(
            tokens_hbm.at[rows_of(i, CHUNK)],
            tok.at[pl.ds(pl.multiple_of(HALO + i * CHUNK, HALO), CHUNK)],
            tok_sem.at[i],
        )

    def token_rows(i):
        return tok[pl.ds(pl.multiple_of(HALO + i * CHUNK, HALO), CHUNK), :]

    load_tokens(spans).start()
    for n in range(wides):
        for copy in load_weights(n):
            copy.start()
    for copy in small:
        copy.start()

    barrier = pltpu.get_barrier_semaphore()

    @pl.loop(1, n_req)
    def _(j):
        pl.semaphore_signal(barrier, inc=1, device_id={"req": peer(j)}, device_id_type=MESH)

    for side in (left, right):
        pl.semaphore_signal(barrier, inc=1, device_id={"ch": side}, device_id_type=MESH)

    def halo_copy():
        return pltpu.make_async_remote_copy(
            src_ref=tokens_hbm.at[pl.ds(SPAN_ROWS - HALO, HALO)],
            dst_ref=tok.at[pl.ds(0, HALO)],
            send_sem=halo_send_sem,
            recv_sem=halo_recv_sem,
            device_id={"req": peer(1)},
            device_id_type=MESH,
        )

    def first_copy(c, side):
        source, target, device = ((send_r, recv_l, right), (send_l, recv_r, left))[side]
        return pltpu.make_async_remote_copy(
            src_ref=source.at[c],
            dst_ref=target.at[c],
            send_sem=one_send.at[c, side],
            recv_sem=one_recv.at[c, side],
            device_id={"ch": device},
            device_id_type=MESH,
        )

    def second_copy(c, side):
        source, target, device = ((send2_r, recv2_l, right), (send2_l, recv2_r, left))[side]
        return pltpu.make_async_remote_copy(
            src_ref=source.at[c],
            dst_ref=target.at[c],
            send_sem=two_send.at[c, side],
            recv_sem=two_recv.at[c, side],
            device_id={"ch": device},
            device_id_type=MESH,
        )

    def a2a_copy(j):
        return pltpu.make_async_remote_copy(
            src_ref=a2a_send.at[peer(j)],
            dst_ref=a2a_recv.at[me],
            send_sem=a2a_send_sem.at[j],
            recv_sem=a2a_recv_sem.at[j],
            device_id={"req": peer(j)},
            device_id_type=MESH,
        )

    def sum_copy(j):
        return pltpu.make_async_remote_copy(
            src_ref=sum_send,
            dst_ref=sum_recv.at[j - 1],
            send_sem=sum_send_sem.at[j - 1],
            recv_sem=sum_recv_sem.at[j - 1],
            device_id={"req": peer(j)},
            device_id_type=MESH,
        )

    def spread_accepted():
        across = lax.broadcasted_iota(jnp.int32, (requests, requests), 1)
        down = lax.broadcasted_iota(jnp.int32, (requests, requests), 0)
        column = jnp.sum(
            jnp.where(across == down, accepted_ref[...], 0), axis=1, keepdims=True
        )
        acc_b[...] = jnp.broadcast_to(column, (requests, BLOCK))

    spread_accepted()

    firsts = [jnp.int32(0)]
    for i in range(span_ref.shape[0] - 1):
        firsts.append(firsts[-1] + span_ref[i])

    def project(tokens, n):
        at = slice(n * WIDE, (n + 1) * WIDE)
        proj[:, at] = jnp.dot(tokens, w_cat[:, at], preferred_element_type=F32)

    def gelu(u):
        return (0.5 * u) * (1.0 + jnp.tanh(u * (0.7978845608028654 + 0.035677408136300125 * (u * u))))

    def gates(conv, b):
        both = jnp.dot(conv.astype(BF16), gw[b], preferred_element_type=F32)
        rate_gate = 0.5 + 0.5 * jnp.tanh(0.5 * both[:, :BLOCK])
        input_gate = 0.5 + 0.5 * jnp.tanh(0.5 * both[:, BLOCK:])
        y = rates[0:1, lanes(b)] * rate_gate
        series = SERIES[-1]
        for term in SERIES[-2::-1]:
            series = series * y + term
        z = y * series
        drive = z * lax.rsqrt(jnp.maximum(z, 1e-37)) * input_gate * conv
        return jnp.exp(-0.5 * y), drive

    def spread():
        return jnp.concatenate([hidden[b] for b in range(blocks)], 1)

    def project_out(c, gated, opening=False):
        def shares(k):
            at = slice(k * chans, (k + 2) * chans)
            both = jnp.dot(gated, w_out[:, at], preferred_element_type=F32)
            return both[:, :chans].astype(BF16), both[:, chans:].astype(BF16)

        to_far, to_right = shares(0)
        send_r[c, pl.ds(0, HALF)] = to_far[:HALF]
        send_l[c, pl.ds(0, HALF)] = to_far[HALF:]
        stash_r[c] = to_right[:HALF]
        send_r[c, pl.ds(HALF, HALF)] = to_right[HALF:]
        if opening:
            pl.semaphore_wait(barrier, n_req - 1 + 2)
        first_copy(c, 0).start()
        to_left, to_own = shares(2)
        send_l[c, pl.ds(HALF, HALF)] = to_left[:HALF]
        stash_l[c] = to_left[HALF:]
        first_copy(c, 1).start()
        own[c] = to_own
        if opening:
            halo_copy().start()

    def pass_on(c):
        first_copy(c, 0).wait_recv()
        send2_r[c] = (recv_l[c, pl.ds(0, HALF)].astype(F32) + stash_r[c].astype(F32)).astype(BF16)
        second_copy(c, 0).start()
        first_copy(c, 1).wait_recv()
        send2_l[c] = (recv_r[c, pl.ds(0, HALF)].astype(F32) + stash_l[c].astype(F32)).astype(BF16)
        second_copy(c, 1).start()

    def finish(c):
        second_copy(c, 0).wait_recv()
        second_copy(c, 1).wait_recv()
        upper = own[c, pl.ds(0, HALF)].astype(F32) + recv2_l[c].astype(F32)
        lower = own[c, pl.ds(HALF, HALF)].astype(F32) + recv2_r[c].astype(F32)
        upper = upper + recv_r[c, pl.ds(HALF, HALF)].astype(F32)
        lower = lower + recv_l[c, pl.ds(HALF, HALF)].astype(F32)
        base = jnp.where(c < drafts, SPAN_ROWS + c * CHUNK, (c - drafts) * CHUNK)
        mout[pl.ds(pl.multiple_of(base, HALF), HALF), :] = upper.astype(BF16)
        mout[pl.ds(pl.multiple_of(base + HALF, HALF), HALF), :] = lower.astype(BF16)

    step = lax.broadcasted_iota(jnp.int32, (CHUNK, BLOCK), 0)
    offset = (step % GROUP) * DRAFT + step // GROUP

    def edge_rows():
        halo_copy().wait_recv()
        edge = tok[pl.ds(0, HALO), :]
        for b in range(blocks):
            columns = w_cat[:, b * BLOCK : (b + 1) * BLOCK]
            inner_s[b, pl.ds(0, HALO)] = (
                jnp.dot(edge, columns, preferred_element_type=F32).astype(BF16).astype(F32)
            )

    def span_chunk(q, following):
        for b in range(blocks):
            inner_s[b, pl.ds(pl.multiple_of(HALO + q * CHUNK, HALO), CHUNK)] = (
                proj[:, b * BLOCK : (b + 1) * BLOCK].astype(BF16).astype(F32)
            )
        branch_s[rows_of(q, CHUNK), :] = gelu(proj[:, chans:])
        position = me * SPAN_ROWS + q * CHUNK + offset
        begin = jnp.zeros((CHUNK, BLOCK), jnp.int32)
        for first in firsts:
            begin = jnp.where(first <= position, first, begin)
        age = position - begin
        tokens = token_rows(following)
        base = HALO - HIST + q * CHUNK
        for b in range(blocks):
            project(tokens, b)
            rows = [
                inner_s[b, pl.ds(base + i, GROUP, stride=DRAFT), :] for i in range(DRAFT + HIST)
            ]
            x = jnp.concatenate(rows, 0)
            conv = conv_ref[0:1, lanes(b)] * x[HIST * GROUP : HIST * GROUP + CHUNK]
            for k in range(1, CONV):
                at = (HIST - k) * GROUP
                term = conv_ref[k : k + 1, lanes(b)] * x[at : at + CHUNK]
                conv = conv + jnp.where(age >= k, term, 0.0)
            decay, drive = gates(conv, b)
            decay = jnp.where(age > 0, decay, 0.0)
            h = jnp.zeros((GROUP, BLOCK), F32)
            a = jnp.ones((GROUP, BLOCK), F32)
            for t in range(DRAFT):
                part = slice(t * GROUP, (t + 1) * GROUP)
                h = decay[part] * h + drive[part]
                a = decay[part] * a
                at = pl.ds(pl.multiple_of(q * CHUNK + t * GROUP, GROUP), GROUP)
                local[at, lanes(b)] = h
                decays[at, lanes(b)] = a
            ends_a[rows_of(q, GROUP), lanes(b)] = a
            ends_h[rows_of(q, GROUP), lanes(b)] = h

    def link(s, carry):
        product, value = carry
        at = pl.ds(s, 1)
        a = ends_a[at, :]
        h = ends_h[at, :]
        ends_a[at, :] = product
        ends_h[at, :] = value
        return (a * product, a * value + h)

    def send_sums():
        product, value = lax.fori_loop(
            0, spans * GROUP, link, (jnp.ones((1, chans), F32), jnp.zeros((1, chans), F32))
        )
        sum_send[...] = jnp.zeros_like(sum_send)
        sum_send[0:1, :] = product
        sum_send[1:2, :] = value
        for j in range(1, BACK + 1):
            sum_copy(j).start()

    def draft_chunk(c, following, opening=False):
        for b in range(blocks):
            inner[b] = proj[:, b * BLOCK : (b + 1) * BLOCK].astype(BF16).astype(F32)
        branch[...] = gelu(proj[:, chans:])
        members = rows_of(c, GROUP)
        accepted = acc_b[members, :]
        chosen = [accepted == t + 1 for t in range(DRAFT)]
        tokens = token_rows(following)
        for b in range(blocks):
            project(tokens, b)
            rows = [cached_f[j, members, lanes(b)] for j in range(HIST)]
            rows += [inner[b, pl.ds(t, GROUP, stride=DRAFT), :] for t in range(DRAFT)]
            x = jnp.concatenate(rows, 0)
            conv = 0.0
            for k in range(CONV):
                at = (HIST - k) * GROUP
                conv = conv + conv_ref[k : k + 1, lanes(b)] * x[at : at + CHUNK]
            decay, drive = gates(conv, b)
            h = state[members, lanes(b)]
            picked = [jnp.zeros((GROUP, BLOCK), F32) for _ in range(1 + HIST)]
            for t in range(DRAFT):
                part = slice(t * GROUP, (t + 1) * GROUP)
                h = decay[part] * h + drive[part]
                hidden[b, pl.ds(t, GROUP, stride=DRAFT), :] = h
                picked[0] = jnp.where(chosen[t], h, picked[0])
                for j in range(HIST):
                    picked[1 + j] = jnp.where(chosen[t], rows[t + 1 + j], picked[1 + j])
            for j in range(1 + HIST):
                at = pl.ds(pl.multiple_of(j * requests + c * GROUP, GROUP), GROUP)
                kept[at, lanes(b)] = picked[j]
        project_out(c, (branch[...] * spread()).astype(BF16), opening)

    load_tokens(spans).wait()
    tokens = token_rows(spans)
    for n in range(wides):
        for copy in load_weights(n):
            copy.wait()
        project(tokens, n)

    for copy in load_out:
        copy.start()
    for q in range(spans):
        load_tokens(q).start()

    @pl.loop(spans + 1, spans + drafts)
    def _(i):
        load_tokens(i).start()

    for copy in small:
        copy.wait()
    cached_f[...] = cached[...].astype(F32)
    rates[0:1, :] = 16.0 * rate_ref[...].reshape(1, chans)
    for copy in load_out:
        copy.wait()
    load_tokens(spans + 1).wait()
    draft_chunk(0, spans + 1, opening=True)

    @pl.loop(0, spans)
    def _(i):
        load_tokens(i).wait()
        draft_chunk(i + 1, i)

        @pl.when(i == 0)
        def _():
            edge_rows()

        @pl.when(i > 0)
        def _():
            pass_on(i - 1)

        load_tokens(spans + 2 + i).wait()
        span_chunk(i, spans + 2 + i)

    send_sums()

    @pl.loop(spans + 1, drafts)
    def _(c):
        @pl.when(c < drafts - 1)
        def _():
            load_tokens(spans + 1 + c).wait()

        draft_chunk(c, spans + jnp.minimum(c + 1, drafts - 1))
        pass_on(c - lag)

    owner_row = owner_ref[...]
    across = lax.broadcasted_iota(jnp.int32, (requests, requests), 1)
    down = lax.broadcasted_iota(jnp.int32, (requests, requests), 0)
    owner_column = jnp.sum(jnp.where(across == down, owner_row, 0), axis=1, keepdims=True)
    same = jnp.where(owner_column == owner_row, 1, 0)
    rank_row = jnp.sum(jnp.where(down < across, same, 0), axis=0, keepdims=True)
    slot_row = owner_row * slots + rank_row
    kinds = 1 + HIST
    tall = n_req * kinds * slots
    item = lax.broadcasted_iota(jnp.int32, (tall, requests), 0)
    slot_of = (item // (kinds * slots)) * slots + item % slots
    kind_of = (item // slots) % kinds
    hit = jnp.where(slot_of == slot_row, 1.0, 0.0)
    total = jnp.zeros((tall, chans), F32)
    for j in range(kinds):
        pick = jnp.where(kind_of == j, hit, 0.0).astype(BF16)
        total = total + jnp.dot(
            pick,
            kept[pl.ds(j * requests, requests), :].astype(BF16),
            preferred_element_type=F32,
        )
    a2a_send[...] = total.astype(BF16).reshape(n_req, kinds * slots, chans)

    @pl.loop(1, n_req)
    def _(j):
        a2a_copy(j).start()

    local_copy = pltpu.make_async_copy(a2a_send.at[me], a2a_recv.at[me], a2a_send_sem.at[0])
    local_copy.start()

    @pl.loop(drafts - lag, drafts)
    def _(c):
        pass_on(c)

    for j in range(1, BACK + 1):
        sum_copy(j).wait_recv()
    entering = sum_recv[BACK - 1, 1:2, :]
    for j in range(BACK - 2, -1, -1):
        entering = sum_recv[j, 0:1, :] * entering + sum_recv[j, 1:2, :]

    @pl.loop(0, spans)
    def _(q):
        carry = ends_h[rows_of(q, GROUP), :] + ends_a[rows_of(q, GROUP), :] * entering
        for t in range(DRAFT):
            at = pl.ds(pl.multiple_of(q * CHUNK + t * GROUP, GROUP), GROUP)
            h = local[at, :] + decays[at, :] * carry
            for b in range(blocks):
                hidden[b, pl.ds(t, GROUP, stride=DRAFT), :] = h[:, b * BLOCK : (b + 1) * BLOCK]
        project_out(drafts + q, (branch_s[rows_of(q, CHUNK), :] * spread()).astype(BF16))

        @pl.when(q >= lag)
        def _():
            pass_on(drafts + q - lag)

    local_copy.wait()

    @pl.loop(1, n_req)
    def _(j):
        a2a_copy(j).wait_recv()

    got = a2a_recv[...]
    ost[...] = got[:, :slots].astype(F32).reshape(n_req * slots, chans)
    for j in range(HIST):
        oin[j] = (
            got[:, (1 + j) * slots : (2 + j) * slots].astype(F32).reshape(n_req * slots, chans).astype(BF16)
        )
    @pl.loop(drafts + max(spans - lag, 0), drafts + spans)
    def _(c):
        pass_on(c)

    @pl.loop(0, drafts + spans)
    def _(c):
        finish(c)

    halo_copy().wait_send()
    for j in range(1, BACK + 1):
        sum_copy(j).wait_send()

    @pl.loop(1, n_req)
    def _(j):
        a2a_copy(j).wait_send()

    @pl.loop(0, drafts + spans)
    def _(c):
        for side in range(2):
            first_copy(c, side).wait_send()
            second_copy(c, side).wait_send()


def write_out(*refs):
    sources, targets, sems = refs[:3], refs[3:6], refs[6]
    copies = [
        pltpu.make_async_copy(source, target, sems.at[i])
        for i, (source, target) in enumerate(zip(sources, targets))
    ]
    for copy in copies:
        copy.start()
    for copy in copies:
        copy.wait()


def per_device(
    n_req,
    n_ch,
    tokens,
    w_in,
    w_gate,
    gate_a,
    gate_i,
    conv_w,
    decay_rate,
    w_out,
    cached_state,
    cached_inputs,
    span_lengths,
    accepted,
    owner,
):
    rows, width = tokens.shape
    chans = w_in.shape[1]
    blocks = chans // BLOCK
    requests = accepted.shape[0]
    slots = 2 * requests // n_req
    kinds = 1 + HIST
    drafts = requests * DRAFT // CHUNK
    spans = SPAN_ROWS // CHUNK
    chunks = drafts + spans
    lag = min(2, spans)
    vmem, anywhere, smem = (
        pl.BlockSpec(memory_space=pltpu.VMEM),
        pl.BlockSpec(memory_space=pl.ANY),
        pl.BlockSpec(memory_space=pltpu.SMEM),
    )
    dma = pltpu.SemaphoreType.DMA
    mixed, ostate, oin = pl.pallas_call(
        functools.partial(kernel, lag, n_req, n_ch),
        out_shape=(
            pltpu.VMEM((rows, chans), BF16),
            pltpu.VMEM((n_req * slots, chans), F32),
            pltpu.VMEM((HIST, n_req * slots, chans), BF16),
        ),
        in_specs=[smem, vmem, vmem, vmem, vmem] + [anywhere] * 8,
        out_specs=(vmem, vmem, vmem),
        scratch_shapes=[
            pltpu.VMEM((width, 2 * chans), BF16),
            pltpu.VMEM((chans, n_ch * chans), BF16),
            pltpu.VMEM((HALO + rows, width), BF16),
            pltpu.VMEM((blocks, BLOCK, 2 * BLOCK), BF16),
            pltpu.VMEM((requests, chans), F32),
            pltpu.VMEM((HIST, requests, chans), BF16),
            pltpu.VMEM((HIST, requests, chans), F32),
            pltpu.VMEM((CHUNK, 2 * chans), F32),
            pltpu.VMEM((blocks, CHUNK, BLOCK), F32),
            pltpu.VMEM((CHUNK, chans), F32),
            pltpu.VMEM((blocks, CHUNK, BLOCK), F32),
            pltpu.VMEM((kinds * requests, chans), F32),
            pltpu.VMEM((requests, BLOCK), jnp.int32),
            pltpu.VMEM((blocks, HALO + SPAN_ROWS, BLOCK), F32),
            pltpu.VMEM((SPAN_ROWS, chans), F32),
            pltpu.VMEM((SPAN_ROWS, chans), F32),
            pltpu.VMEM((SPAN_ROWS, chans), F32),
            pltpu.VMEM((spans * GROUP, chans), F32),
            pltpu.VMEM((spans * GROUP, chans), F32),
            pltpu.VMEM((8, chans), F32),
            pltpu.VMEM((BACK, 8, chans), F32),
            pltpu.VMEM((chunks, CHUNK, chans), BF16),
            pltpu.VMEM((chunks, HALF, chans), BF16),
            pltpu.VMEM((chunks, HALF, chans), BF16),
            pltpu.VMEM((chunks, CHUNK, chans), BF16),
            pltpu.VMEM((chunks, CHUNK, chans), BF16),
            pltpu.VMEM((chunks, CHUNK, chans), BF16),
            pltpu.VMEM((chunks, CHUNK, chans), BF16),
            pltpu.VMEM((chunks, HALF, chans), BF16),
            pltpu.VMEM((chunks, HALF, chans), BF16),
            pltpu.VMEM((chunks, HALF, chans), BF16),
            pltpu.VMEM((chunks, HALF, chans), BF16),
            pltpu.VMEM((n_req, kinds * slots, chans), BF16),
            pltpu.VMEM((n_req, kinds * slots, chans), BF16),
            pltpu.VMEM((8, chans), F32),
            dma((9,)),
            dma((2 * chans // WIDE, 2)),
            dma((chunks,)),
            dma,
            dma,
            dma((BACK,)),
            dma((BACK,)),
            dma((chunks, 2)),
            dma((chunks, 2)),
            dma((chunks, 2)),
            dma((chunks, 2)),
            dma((n_req,)),
            dma((n_req,)),
        ],
        compiler_params=pltpu.CompilerParams(
            collective_id=0, has_side_effects=True, vmem_limit_bytes=52 * 1024 * 1024
        ),
        name="griffin",
    )(
        span_lengths,
        accepted.reshape(1, requests),
        owner.reshape(1, requests),
        conv_w,
        decay_rate,
        tokens,
        w_in,
        w_gate,
        gate_a,
        gate_i,
        w_out,
        cached_state,
        jnp.transpose(cached_inputs, (1, 0, 2)),
    )
    mixed, ostate, oin = pl.pallas_call(
        write_out,
        out_shape=tuple(jax.ShapeDtypeStruct(a.shape, a.dtype) for a in (mixed, ostate, oin)),
        in_specs=[vmem] * 3,
        out_specs=(anywhere,) * 3,
        scratch_shapes=[dma((3,))],
        name="write_out",
    )(*(pltpu.with_memory_space_constraint(a, pltpu.VMEM) for a in (mixed, ostate, oin)))
    return (
        mixed,
        ostate.reshape(1, n_req * slots, chans),
        jnp.transpose(oin, (1, 0, 2)).reshape(1, n_req * slots, HIST, chans),
    )


def solution(mesh):
    return jax.shard_map(
        functools.partial(per_device, mesh.shape["req"], mesh.shape["ch"]),
        mesh=mesh,
        in_specs=(
            P("req", None),
            P(None, "ch"),
            P(None, "ch"),
            P("ch", None, None),
            P("ch", None, None),
            P(None, "ch"),
            P("ch"),
            P("ch", None),
            P("req", "ch"),
            P("req", None, "ch"),
            P(),
            P("req"),
            P("req", None),
        ),
        out_specs=(P("req", "ch"), P("req", None, "ch"), P("req", None, None, "ch")),
        check_vma=False,
    )
```

```python
import functools

import jax
import jax.numpy as jnp
from jax import lax
from jax.experimental import pallas as pl
from jax.experimental.pallas import tpu as pltpu
from jax.sharding import PartitionSpec as P

CONV = 4
HIST = CONV - 1
DRAFT = 16
SPAN_ROWS = 512
BLOCK = 128
WIDE = 256
CHUNK = 128
HALF = CHUNK // 2
GROUP = CHUNK // DRAFT
HALO = 16
BACK = 4
RING = 6
MESH = pl.DeviceIdType.MESH
F32 = jnp.float32
BF16 = jnp.bfloat16
SERIES = (0.99999999, -0.49999941, 0.16665585, -0.04159356, 0.00810764, -0.00105947)


def lanes(b):
    return pl.ds(pl.multiple_of(b * BLOCK, BLOCK), BLOCK)


def rows_of(c, count):
    return pl.ds(pl.multiple_of(c * count, count), count)


def kernel(
    lag,
    n_req,
    n_ch,
    span_ref,
    accepted_ref,
    owner_ref,
    conv_ref,
    rate_ref,
    tokens_hbm,
    w_in_hbm,
    w_gate_hbm,
    gate_a_hbm,
    gate_i_hbm,
    w_out_hbm,
    state_hbm,
    cached_hbm,
    mout,
    ost,
    oin,
    w_cat,
    w_out,
    tok,
    gw,
    state,
    cached,
    cached_f,
    proj,
    inner,
    branch,
    hidden,
    kept,
    acc_b,
    inner_s,
    branch_s,
    local,
    decays,
    ends_a,
    ends_h,
    sum_send,
    sum_recv,
    own,
    stash_p,
    stash_q,
    send_p,
    send_q,
    recv_p,
    recv_q,
    send2_p,
    send2_q,
    recv2_p,
    recv2_q,
    gated_x,
    gated_r,
    pair_send,
    pair_recv,
    pair_own,
    last_send,
    last_recv,
    a2a_send,
    a2a_recv,
    rates,
    load_sem,
    w_sem,
    tok_sem,
    halo_send_sem,
    halo_recv_sem,
    sum_send_sem,
    sum_recv_sem,
    one_send,
    one_recv,
    two_send,
    two_recv,
    a2a_send_sem,
    a2a_recv_sem,
    piece_sem,
    spread_send,
    spread_recv,
    core_send,
    core_recv,
    pair_send_sem,
    pair_recv_sem,
):
    chans = w_in_hbm.shape[1]
    blocks = chans // BLOCK
    requests = accepted_ref.shape[1]
    slots = 2 * requests // n_req
    drafts = requests * DRAFT // CHUNK
    spans = SPAN_ROWS // CHUNK
    wides = 2 * chans // WIDE
    me = lax.axis_index("req")
    place = lax.axis_index("ch")
    odd = lax.rem(place, 2)
    mate = place + 1 - 2 * odd
    other = lax.rem(place + n_ch - 1 + 2 * odd, n_ch)
    far = lax.rem(place + 2, n_ch)
    mine = lax.rem((place + 1) // 2, 2)
    groups = n_req // n_ch
    piece_rows = chans // groups
    kind = me // groups
    piece = lax.rem(me, groups)

    def peer(j):
        return lax.rem(me + j, n_req)

    barrier = pltpu.get_barrier_semaphore()

    @pl.loop(1, n_req)
    def _(j):
        pl.semaphore_signal(barrier, inc=1, device_id={"req": peer(j)}, device_id_type=MESH)

    for side in (mate, other):
        pl.semaphore_signal(barrier, inc=1, device_id={"ch": side}, device_id_type=MESH)

    def load_weights(n):
        pieces = []
        for k, source in enumerate((w_in_hbm, w_gate_hbm)):
            low, high = max(n * WIDE, k * chans), min((n + 1) * WIDE, (k + 1) * chans)
            if low < high:
                pieces.append(
                    pltpu.make_async_copy(
                        source.at[:, pl.ds(low - k * chans, high - low)],
                        w_cat.at[:, pl.ds(low, high - low)],
                        w_sem.at[n, k],
                    )
                )
        return pieces

    small = [
        pltpu.make_async_copy(gate_a_hbm, gw.at[:, :, pl.ds(0, BLOCK)], load_sem.at[0]),
        pltpu.make_async_copy(gate_i_hbm, gw.at[:, :, pl.ds(BLOCK, BLOCK)], load_sem.at[1]),
        pltpu.make_async_copy(state_hbm, state, load_sem.at[2]),
        pltpu.make_async_copy(cached_hbm, cached, load_sem.at[3]),
    ]
    load_out = []
    for k, source in enumerate((far, other, place, mate)):
        columns = pl.ds(pl.multiple_of(source * chans, BLOCK), chans)
        load_out.append(
            pltpu.make_async_copy(
                w_out_hbm.at[:, columns], w_out.at[pl.ds(0, chans), pl.ds(k * chans, chans)], load_sem.at[4 + k]
            )
        )

    def load_tokens(i):
        return pltpu.make_async_copy(
            tokens_hbm.at[rows_of(i, CHUNK)],
            tok.at[pl.ds(pl.multiple_of(HALO + i * CHUNK, HALO), CHUNK)],
            tok_sem.at[i],
        )

    def token_rows(i):
        return tok[pl.ds(pl.multiple_of(HALO + i * CHUNK, HALO), CHUNK), :]

    load_tokens(spans).start()
    for n in range(wides):
        for copy in load_weights(n):
            copy.start()
    for copy in small:
        copy.start()

    def halo_copy():
        return pltpu.make_async_remote_copy(
            src_ref=tokens_hbm.at[pl.ds(SPAN_ROWS - HALO, HALO)],
            dst_ref=tok.at[pl.ds(0, HALO)],
            send_sem=halo_send_sem,
            recv_sem=halo_recv_sem,
            device_id={"req": peer(1)},
            device_id_type=MESH,
        )

    def first_copy(c, side):
        source, target, device = ((send_p, recv_p, mate), (send_q, recv_q, other))[side]
        return pltpu.make_async_remote_copy(
            src_ref=source.at[c],
            dst_ref=target.at[c],
            send_sem=one_send.at[c, side],
            recv_sem=one_recv.at[c, side],
            device_id={"ch": device},
            device_id_type=MESH,
        )

    def second_copy(c, side):
        source, target, device = ((send2_p, recv2_p, mate), (send2_q, recv2_q, other))[side]
        return pltpu.make_async_remote_copy(
            src_ref=source.at[c],
            dst_ref=target.at[c],
            send_sem=two_send.at[c, side],
            recv_sem=two_recv.at[c, side],
            device_id={"ch": device},
            device_id_type=MESH,
        )

    def a2a_copy(j):
        return pltpu.make_async_remote_copy(
            src_ref=a2a_send.at[peer(j)],
            dst_ref=a2a_recv.at[me],
            send_sem=a2a_send_sem.at[j],
            recv_sem=a2a_recv_sem.at[j],
            device_id={"req": peer(j)},
            device_id_type=MESH,
        )

    def sum_copy(j):
        return pltpu.make_async_remote_copy(
            src_ref=sum_send,
            dst_ref=sum_recv.at[j - 1],
            send_sem=sum_send_sem.at[j - 1],
            recv_sem=sum_recv_sem.at[j - 1],
            device_id={"req": peer(j)},
            device_id_type=MESH,
        )

    def spread_accepted():
        across = lax.broadcasted_iota(jnp.int32, (requests, requests), 1)
        down = lax.broadcasted_iota(jnp.int32, (requests, requests), 0)
        column = jnp.sum(
            jnp.where(across == down, accepted_ref[...], 0), axis=1, keepdims=True
        )
        acc_b[...] = jnp.broadcast_to(column, (requests, BLOCK))

    spread_accepted()

    firsts = [jnp.int32(0)]
    for i in range(span_ref.shape[0] - 1):
        firsts.append(firsts[-1] + span_ref[i])

    def project(tokens, n):
        at = slice(n * WIDE, (n + 1) * WIDE)
        proj[:, at] = jnp.dot(tokens, w_cat[:, at], preferred_element_type=F32)

    def gelu(u):
        return (0.5 * u) * (1.0 + jnp.tanh(u * (0.7978845608028654 + 0.035677408136300125 * (u * u))))

    def gates(conv, b):
        both = jnp.dot(conv.astype(BF16), gw[b], preferred_element_type=F32)
        rate_gate = 0.5 + 0.5 * jnp.tanh(0.5 * both[:, :BLOCK])
        input_gate = 0.5 + 0.5 * jnp.tanh(0.5 * both[:, BLOCK:])
        y = rates[0:1, lanes(b)] * rate_gate
        series = SERIES[-1]
        for term in SERIES[-2::-1]:
            series = series * y + term
        z = y * series
        drive = z * lax.rsqrt(jnp.maximum(z, 1e-37)) * input_gate * conv
        return jnp.exp(-0.5 * y), drive

    def spread():
        return jnp.concatenate([hidden[b] for b in range(blocks)], 1)

    def project_out(c, gated, opening=False):
        def shares(k):
            at = slice(k * chans, (k + 2) * chans)
            both = jnp.dot(gated, w_out[pl.ds(0, chans), at], preferred_element_type=F32)
            return both[:, :chans].astype(BF16), both[:, chans:].astype(BF16)

        to_far, to_other = shares(0)
        send_p[c, pl.ds(0, HALF)] = to_far[:HALF]
        send_q[c, pl.ds(0, HALF)] = to_far[HALF:]
        stash_q[c] = to_other[:HALF]
        send_q[c, pl.ds(HALF, HALF)] = to_other[HALF:]
        if opening:
            pl.semaphore_wait(barrier, n_req - 1 + 2)
            halo_copy().start()
            piece_copy().start()
        first_copy(c, 1).start()
        to_own, to_mate = shares(2)
        send_p[c, pl.ds(HALF, HALF)] = to_mate[:HALF]
        stash_p[c] = to_mate[HALF:]
        first_copy(c, 0).start()
        own[c] = to_own

    def pass_on(c):
        first_copy(c, 0).wait_recv()
        send2_q[c] = (recv_p[c, pl.ds(0, HALF)].astype(F32) + stash_q[c].astype(F32)).astype(BF16)
        second_copy(c, 1).start()
        first_copy(c, 1).wait_recv()
        send2_p[c] = (recv_q[c, pl.ds(0, HALF)].astype(F32) + stash_p[c].astype(F32)).astype(BF16)
        second_copy(c, 0).start()

    def slot_of_kind(device):
        step = lax.rem(kind - device + n_ch, n_ch)
        parity = lax.rem(device, 2)
        turned = lax.rem(step + parity * (n_ch - 2 * step) + n_ch, n_ch)
        return pl.multiple_of(lax.rem(turned + 2, n_ch) * chans, BLOCK)

    def piece_copy():
        rows = pl.multiple_of(piece * piece_rows, 16)
        columns = pl.multiple_of(kind * chans, BLOCK)
        return pltpu.make_async_remote_copy(
            src_ref=w_out_hbm.at[pl.ds(rows, piece_rows), pl.ds(columns, chans)],
            dst_ref=w_out.at[pl.ds(pl.multiple_of(chans + rows, 16), piece_rows), pl.ds(slot_of_kind(mate), chans)],
            send_sem=piece_sem.at[0],
            recv_sem=piece_sem.at[1],
            device_id={"ch": mate},
            device_id_type=MESH,
        )

    def spread_copy(j):
        rows = pl.multiple_of(chans + piece * piece_rows, 16)
        part = w_out.at[pl.ds(rows, piece_rows), pl.ds(slot_of_kind(place), chans)]
        return pltpu.make_async_remote_copy(
            src_ref=part,
            dst_ref=part,
            send_sem=spread_send.at[j],
            recv_sem=spread_recv.at[j],
            device_id={"req": peer(2 * j)},
            device_id_type=MESH,
        )

    def core_copy(g):
        rows = pl.multiple_of(chans + (2 * g + lax.rem(me, 2)) * piece_rows, 16)
        part = w_out.at[pl.ds(rows, piece_rows)]
        return pltpu.make_async_remote_copy(
            src_ref=part,
            dst_ref=part,
            send_sem=core_send.at[g],
            recv_sem=core_recv.at[g],
            device_id={"req": me + 1 - 2 * lax.rem(me, 2)},
            device_id_type=MESH,
        )

    def spread_pieces():
        piece_copy().wait_recv()

        @pl.loop(1, n_req // 2)
        def _(j):
            spread_copy(j).start()

    def swap_cores():
        @pl.loop(1, n_req // 2)
        def _(j):
            spread_copy(j).wait_recv()

        for g in range(groups // 2):
            core_copy(g).start()

    def pair_copy(stage, j):
        source, target, device = (
            (gated_x.at[j, 1 - mine], gated_r.at[j], mate),
            (pair_send.at[0, j], pair_recv.at[0, j], other),
            (pair_send.at[1, j], pair_recv.at[1, j], other),
            (last_send.at[j], last_recv.at[j], mate),
        )[stage]
        return pltpu.make_async_remote_copy(
            src_ref=source,
            dst_ref=target,
            send_sem=pair_send_sem.at[stage, j],
            recv_sem=pair_recv_sem.at[stage, j],
            device_id={"ch": device},
            device_id_type=MESH,
        )

    def pair_project(j):
        pair_copy(0, j).wait_recv()
        both = jnp.concatenate([gated_x[j, mine], gated_r[j]], 1)
        outer = jnp.dot(both, w_out[:, : 2 * chans], preferred_element_type=F32)
        pair_send[0, j] = outer[:, :chans].astype(BF16)
        pair_copy(1, j).start()
        pair_send[1, j] = outer[:, chans:].astype(BF16)
        pair_copy(2, j).start()
        pair_own[j] = jnp.dot(both, w_out[:, 2 * chans :], preferred_element_type=F32)

    def pair_rows(j, chunk):
        first = RING + 2 * j
        base = jnp.where(first < drafts, SPAN_ROWS + first * CHUNK, (first - drafts) * CHUNK)
        return pl.ds(pl.multiple_of(base + chunk * CHUNK, CHUNK), CHUNK)

    def pair_sum(j):
        pair_copy(1, j).wait_recv()
        last_send[j] = (pair_own[j, :, chans:] + pair_recv[0, j].astype(F32)).astype(BF16)
        pair_copy(3, j).start()

    def pair_keep(j):
        pair_copy(2, j).wait_recv()
        total = pair_own[j, :, :chans] + pair_recv[1, j].astype(F32)
        mout[pair_rows(j, mine), :] = total.astype(BF16)

    def pair_finish(j):
        pair_copy(3, j).wait_recv()
        mout[pair_rows(j, 1 - mine), :] = last_recv[j]

    def finish(c):
        second_copy(c, 0).wait_recv()
        second_copy(c, 1).wait_recv()
        upper = own[c, pl.ds(0, HALF)].astype(F32) + recv2_q[c].astype(F32)
        lower = own[c, pl.ds(HALF, HALF)].astype(F32) + recv2_p[c].astype(F32)
        upper = upper + recv_p[c, pl.ds(HALF, HALF)].astype(F32)
        lower = lower + recv_q[c, pl.ds(HALF, HALF)].astype(F32)
        base = SPAN_ROWS + c * CHUNK
        mout[pl.ds(pl.multiple_of(base, HALF), HALF), :] = upper.astype(BF16)
        mout[pl.ds(pl.multiple_of(base + HALF, HALF), HALF), :] = lower.astype(BF16)

    step = lax.broadcasted_iota(jnp.int32, (CHUNK, BLOCK), 0)
    offset = (step % GROUP) * DRAFT + step // GROUP

    def edge_rows():
        halo_copy().wait_recv()
        edge = tok[pl.ds(0, HALO), :]
        for b in range(blocks):
            columns = w_cat[:, b * BLOCK : (b + 1) * BLOCK]
            inner_s[b, pl.ds(0, HALO)] = (
                jnp.dot(edge, columns, preferred_element_type=F32).astype(BF16).astype(F32)
            )

    def span_chunk(q, following):
        for b in range(blocks):
            inner_s[b, pl.ds(pl.multiple_of(HALO + q * CHUNK, HALO), CHUNK)] = (
                proj[:, b * BLOCK : (b + 1) * BLOCK].astype(BF16).astype(F32)
            )
        branch_s[rows_of(q, CHUNK), :] = gelu(proj[:, chans:])
        position = me * SPAN_ROWS + q * CHUNK + offset
        begin = jnp.zeros((CHUNK, BLOCK), jnp.int32)
        for first in firsts:
            begin = jnp.where(first <= position, first, begin)
        age = position - begin
        tokens = token_rows(following)
        base = HALO - HIST + q * CHUNK
        for b in range(blocks):
            project(tokens, b)
            rows = [
                inner_s[b, pl.ds(base + i, GROUP, stride=DRAFT), :] for i in range(DRAFT + HIST)
            ]
            x = jnp.concatenate(rows, 0)
            conv = conv_ref[0:1, lanes(b)] * x[HIST * GROUP : HIST * GROUP + CHUNK]
            for k in range(1, CONV):
                at = (HIST - k) * GROUP
                term = conv_ref[k : k + 1, lanes(b)] * x[at : at + CHUNK]
                conv = conv + jnp.where(age >= k, term, 0.0)
            decay, drive = gates(conv, b)
            decay = jnp.where(age > 0, decay, 0.0)
            h = jnp.zeros((GROUP, BLOCK), F32)
            a = jnp.ones((GROUP, BLOCK), F32)
            for t in range(DRAFT):
                part = slice(t * GROUP, (t + 1) * GROUP)
                h = decay[part] * h + drive[part]
                a = decay[part] * a
                at = pl.ds(pl.multiple_of(q * CHUNK + t * GROUP, GROUP), GROUP)
                local[at, lanes(b)] = h
                decays[at, lanes(b)] = a
            ends_a[rows_of(q, GROUP), lanes(b)] = a
            ends_h[rows_of(q, GROUP), lanes(b)] = h

    def link(s, carry):
        product, value = carry
        at = pl.ds(s, 1)
        a = ends_a[at, :]
        h = ends_h[at, :]
        ends_a[at, :] = product
        ends_h[at, :] = value
        return (a * product, a * value + h)

    def send_sums():
        product, value = lax.fori_loop(
            0, spans * GROUP, link, (jnp.ones((1, chans), F32), jnp.zeros((1, chans), F32))
        )
        sum_send[...] = jnp.zeros_like(sum_send)
        sum_send[0:1, :] = product
        sum_send[1:2, :] = value
        for j in range(1, BACK + 1):
            sum_copy(j).start()

    def draft_chunk(c, following):
        for b in range(blocks):
            inner[b] = proj[:, b * BLOCK : (b + 1) * BLOCK].astype(BF16).astype(F32)
        branch[...] = gelu(proj[:, chans:])
        members = rows_of(c, GROUP)
        accepted = acc_b[members, :]
        chosen = [accepted == t + 1 for t in range(DRAFT)]
        tokens = token_rows(following)
        for b in range(blocks):
            project(tokens, b)
            rows = [cached_f[j, members, lanes(b)] for j in range(HIST)]
            rows += [inner[b, pl.ds(t, GROUP, stride=DRAFT), :] for t in range(DRAFT)]
            x = jnp.concatenate(rows, 0)
            conv = 0.0
            for k in range(CONV):
                at = (HIST - k) * GROUP
                conv = conv + conv_ref[k : k + 1, lanes(b)] * x[at : at + CHUNK]
            decay, drive = gates(conv, b)
            h = state[members, lanes(b)]
            picked = [jnp.zeros((GROUP, BLOCK), F32) for _ in range(1 + HIST)]
            for t in range(DRAFT):
                part = slice(t * GROUP, (t + 1) * GROUP)
                h = decay[part] * h + drive[part]
                hidden[b, pl.ds(t, GROUP, stride=DRAFT), :] = h
                picked[0] = jnp.where(chosen[t], h, picked[0])
                for j in range(HIST):
                    picked[1 + j] = jnp.where(chosen[t], rows[t + 1 + j], picked[1 + j])
            for j in range(1 + HIST):
                at = pl.ds(pl.multiple_of(j * requests + c * GROUP, GROUP), GROUP)
                kept[at, lanes(b)] = picked[j]
        return (branch[...] * spread()).astype(BF16)

    load_tokens(spans).wait()
    tokens = token_rows(spans)
    for n in range(wides):
        for copy in load_weights(n):
            copy.wait()
        project(tokens, n)

    for copy in load_out:
        copy.start()
    for q in range(spans):
        load_tokens(q).start()

    @pl.loop(spans + 1, spans + drafts)
    def _(i):
        load_tokens(i).start()

    for copy in small:
        copy.wait()
    cached_f[...] = cached[...].astype(F32)
    rates[0:1, :] = 16.0 * rate_ref[...].reshape(1, chans)
    for copy in load_out:
        copy.wait()
    load_tokens(spans + 1).wait()
    project_out(0, draft_chunk(0, spans + 1), opening=True)

    @pl.loop(0, spans)
    def _(i):
        load_tokens(i).wait()
        project_out(i + 1, draft_chunk(i + 1, i))

        @pl.when(i == 0)
        def _():
            edge_rows()
            spread_pieces()

        @pl.when(i > 0)
        def _():
            pass_on(i - 1)

        load_tokens(spans + 2 + i).wait()
        span_chunk(i, spans + 2 + i)

    send_sums()

    def draft_step(c):
        @pl.when(c < drafts - 1)
        def _():
            load_tokens(spans + 1 + c).wait()

        return draft_chunk(c, spans + jnp.minimum(c + 1, drafts - 1))

    @pl.loop(spans + 1, RING)
    def _(c):
        project_out(c, draft_step(c))
        pass_on(c - lag)

    for j in range(1, BACK + 1):
        sum_copy(j).wait_recv()
    entering = sum_recv[BACK - 1, 1:2, :]
    for j in range(BACK - 2, -1, -1):
        entering = sum_recv[j, 0:1, :] * entering + sum_recv[j, 1:2, :]

    @pl.loop(0, spans)
    def _(q):
        carry = ends_h[rows_of(q, GROUP), :] + ends_a[rows_of(q, GROUP), :] * entering
        for t in range(DRAFT):
            at = pl.ds(pl.multiple_of(q * CHUNK + t * GROUP, GROUP), GROUP)
            h = local[at, :] + decays[at, :] * carry
            for b in range(blocks):
                hidden[b, pl.ds(t, GROUP, stride=DRAFT), :] = h[:, b * BLOCK : (b + 1) * BLOCK]
        gated_x[1 + q // 2, lax.rem(q, 2)] = (branch_s[rows_of(q, CHUNK), :] * spread()).astype(BF16)

        @pl.when(lax.rem(q, 2) == 1)
        def _():
            pair_copy(0, 1 + q // 2).start()

    swap_cores()

    @pl.loop(RING, drafts)
    def _(c):
        gated_x[0, c - RING] = draft_step(c)
        pass_on(c - lag)

    pair_copy(0, 0).start()

    for g in range(groups // 2):
        core_copy(g).wait_recv()
    pairs = (drafts + spans - RING) // 2

    @pl.loop(0, pairs)
    def _(j):
        pair_project(lax.rem(j + 1, pairs))

    owner_row = owner_ref[...]
    across = lax.broadcasted_iota(jnp.int32, (requests, requests), 1)
    down = lax.broadcasted_iota(jnp.int32, (requests, requests), 0)
    owner_column = jnp.sum(jnp.where(across == down, owner_row, 0), axis=1, keepdims=True)
    same = jnp.where(owner_column == owner_row, 1, 0)
    rank_row = jnp.sum(jnp.where(down < across, same, 0), axis=0, keepdims=True)
    slot_row = owner_row * slots + rank_row
    kinds = 1 + HIST
    tall = n_req * kinds * slots
    item = lax.broadcasted_iota(jnp.int32, (tall, requests), 0)
    slot_of = (item // (kinds * slots)) * slots + item % slots
    kind_of = (item // slots) % kinds
    hit = jnp.where(slot_of == slot_row, 1.0, 0.0)
    total = jnp.zeros((tall, chans), F32)
    for j in range(kinds):
        pick = jnp.where(kind_of == j, hit, 0.0).astype(BF16)
        total = total + jnp.dot(
            pick,
            kept[pl.ds(j * requests, requests), :].astype(BF16),
            preferred_element_type=F32,
        )
    a2a_send[...] = total.astype(BF16).reshape(n_req, kinds * slots, chans)

    @pl.loop(1, n_req)
    def _(j):
        a2a_copy(j).start()

    local_copy = pltpu.make_async_copy(a2a_send.at[me], a2a_recv.at[me], a2a_send_sem.at[0])
    local_copy.start()

    pair_sum(1)
    pair_keep(1)
    pair_sum(2)

    @pl.loop(0, RING)
    def _(c):
        finish(c)

    pair_keep(2)
    pair_sum(0)

    local_copy.wait()

    @pl.loop(1, n_req)
    def _(j):
        a2a_copy(j).wait_recv()

    got = a2a_recv[...]
    ost[...] = got[:, :slots].astype(F32).reshape(n_req * slots, chans)
    for j in range(HIST):
        oin[j] = (
            got[:, (1 + j) * slots : (2 + j) * slots].astype(F32).reshape(n_req * slots, chans).astype(BF16)
        )
    pair_keep(0)
    for j in (1, 2, 0):
        pair_finish(j)

    halo_copy().wait_send()
    piece_copy().wait_send()

    @pl.loop(1, n_req // 2)
    def _(j):
        spread_copy(j).wait_send()

    for g in range(groups // 2):
        core_copy(g).wait_send()

    @pl.loop(0, pairs)
    def _(j):
        for stage in range(4):
            pair_copy(stage, j).wait_send()

    for j in range(1, BACK + 1):
        sum_copy(j).wait_send()

    @pl.loop(1, n_req)
    def _(j):
        a2a_copy(j).wait_send()

    @pl.loop(0, RING)
    def _(c):
        for side in range(2):
            first_copy(c, side).wait_send()
            second_copy(c, side).wait_send()


def write_out(*refs):
    sources, targets, sems = refs[:3], refs[3:6], refs[6]
    copies = [
        pltpu.make_async_copy(source, target, sems.at[i])
        for i, (source, target) in enumerate(zip(sources, targets))
    ]
    for copy in copies:
        copy.start()
    for copy in copies:
        copy.wait()


def per_device(
    n_req,
    n_ch,
    tokens,
    w_in,
    w_gate,
    gate_a,
    gate_i,
    conv_w,
    decay_rate,
    w_out,
    cached_state,
    cached_inputs,
    span_lengths,
    accepted,
    owner,
):
    rows, width = tokens.shape
    chans = w_in.shape[1]
    blocks = chans // BLOCK
    requests = accepted.shape[0]
    slots = 2 * requests // n_req
    kinds = 1 + HIST
    drafts = requests * DRAFT // CHUNK
    spans = SPAN_ROWS // CHUNK
    chunks = drafts + spans
    pairs = (chunks - RING) // 2
    lag = min(2, spans)
    vmem, anywhere, smem = (
        pl.BlockSpec(memory_space=pltpu.VMEM),
        pl.BlockSpec(memory_space=pl.ANY),
        pl.BlockSpec(memory_space=pltpu.SMEM),
    )
    dma = pltpu.SemaphoreType.DMA
    mixed, ostate, oin = pl.pallas_call(
        functools.partial(kernel, lag, n_req, n_ch),
        out_shape=(
            pltpu.VMEM((rows, chans), BF16),
            pltpu.VMEM((n_req * slots, chans), F32),
            pltpu.VMEM((HIST, n_req * slots, chans), BF16),
        ),
        in_specs=[smem, vmem, vmem, vmem, vmem] + [anywhere] * 8,
        out_specs=(vmem, vmem, vmem),
        scratch_shapes=[
            pltpu.VMEM((width, 2 * chans), BF16),
            pltpu.VMEM((2 * chans, n_ch * chans), BF16),
            pltpu.VMEM((HALO + rows, width), BF16),
            pltpu.VMEM((blocks, BLOCK, 2 * BLOCK), BF16),
            pltpu.VMEM((requests, chans), F32),
            pltpu.VMEM((HIST, requests, chans), BF16),
            pltpu.VMEM((HIST, requests, chans), F32),
            pltpu.VMEM((CHUNK, 2 * chans), F32),
            pltpu.VMEM((blocks, CHUNK, BLOCK), F32),
            pltpu.VMEM((CHUNK, chans), F32),
            pltpu.VMEM((blocks, CHUNK, BLOCK), F32),
            pltpu.VMEM((kinds * requests, chans), F32),
            pltpu.VMEM((requests, BLOCK), jnp.int32),
            pltpu.VMEM((blocks, HALO + SPAN_ROWS, BLOCK), F32),
            pltpu.VMEM((SPAN_ROWS, chans), F32),
            pltpu.VMEM((SPAN_ROWS, chans), F32),
            pltpu.VMEM((SPAN_ROWS, chans), F32),
            pltpu.VMEM((spans * GROUP, chans), F32),
            pltpu.VMEM((spans * GROUP, chans), F32),
            pltpu.VMEM((8, chans), F32),
            pltpu.VMEM((BACK, 8, chans), F32),
            pltpu.VMEM((RING, CHUNK, chans), BF16),
            pltpu.VMEM((RING, HALF, chans), BF16),
            pltpu.VMEM((RING, HALF, chans), BF16),
            pltpu.VMEM((RING, CHUNK, chans), BF16),
            pltpu.VMEM((RING, CHUNK, chans), BF16),
            pltpu.VMEM((RING, CHUNK, chans), BF16),
            pltpu.VMEM((RING, CHUNK, chans), BF16),
            pltpu.VMEM((RING, HALF, chans), BF16),
            pltpu.VMEM((RING, HALF, chans), BF16),
            pltpu.VMEM((RING, HALF, chans), BF16),
            pltpu.VMEM((RING, HALF, chans), BF16),
            pltpu.VMEM((pairs, 2, CHUNK, chans), BF16),
            pltpu.VMEM((pairs, CHUNK, chans), BF16),
            pltpu.VMEM((2, pairs, CHUNK, chans), BF16),
            pltpu.VMEM((2, pairs, CHUNK, chans), BF16),
            pltpu.VMEM((pairs, CHUNK, 2 * chans), F32),
            pltpu.VMEM((pairs, CHUNK, chans), BF16),
            pltpu.VMEM((pairs, CHUNK, chans), BF16),
            pltpu.VMEM((n_req, kinds * slots, chans), BF16),
            pltpu.VMEM((n_req, kinds * slots, chans), BF16),
            pltpu.VMEM((8, chans), F32),
            dma((9,)),
            dma((2 * chans // WIDE, 2)),
            dma((chunks,)),
            dma,
            dma,
            dma((BACK,)),
            dma((BACK,)),
            dma((RING, 2)),
            dma((RING, 2)),
            dma((RING, 2)),
            dma((RING, 2)),
            dma((n_req,)),
            dma((n_req,)),
            dma((2,)),
            dma((n_req // 2,)),
            dma((n_req // 2,)),
            dma((n_req // n_ch // 2,)),
            dma((n_req // n_ch // 2,)),
            dma((4, pairs)),
            dma((4, pairs)),
        ],
        compiler_params=pltpu.CompilerParams(
            collective_id=0, has_side_effects=True, vmem_limit_bytes=52 * 1024 * 1024
        ),
        name="griffin",
    )(
        span_lengths,
        accepted.reshape(1, requests),
        owner.reshape(1, requests),
        conv_w,
        decay_rate,
        tokens,
        w_in,
        w_gate,
        gate_a,
        gate_i,
        w_out,
        cached_state,
        jnp.transpose(cached_inputs, (1, 0, 2)),
    )
    mixed, ostate, oin = pl.pallas_call(
        write_out,
        out_shape=tuple(jax.ShapeDtypeStruct(a.shape, a.dtype) for a in (mixed, ostate, oin)),
        in_specs=[vmem] * 3,
        out_specs=(anywhere,) * 3,
        scratch_shapes=[dma((3,))],
        name="write_out",
    )(*(pltpu.with_memory_space_constraint(a, pltpu.VMEM) for a in (mixed, ostate, oin)))
    return (
        mixed,
        ostate.reshape(1, n_req * slots, chans),
        jnp.transpose(oin, (1, 0, 2)).reshape(1, n_req * slots, HIST, chans),
    )


def solution(mesh):
    return jax.shard_map(
        functools.partial(per_device, mesh.shape["req"], mesh.shape["ch"]),
        mesh=mesh,
        in_specs=(
            P("req", None),
            P(None, "ch"),
            P(None, "ch"),
            P("ch", None, None),
            P("ch", None, None),
            P(None, "ch"),
            P("ch"),
            P("ch", None),
            P("req", "ch"),
            P("req", None, "ch"),
            P(),
            P("req"),
            P("req", None),
        ),
        out_specs=(P("req", "ch"), P("req", None, "ch"), P("req", None, None, "ch")),
        check_vma=False,
    )
```

```python
import functools

import jax
import jax.numpy as jnp
from jax import lax
from jax.experimental import pallas as pl
from jax.experimental.pallas import tpu as pltpu
from jax.sharding import PartitionSpec as P

CONV = 4
HIST = CONV - 1
DRAFT = 16
SPAN_ROWS = 512
BLOCK = 128
WIDE = 256
CHUNK = 128
HALF = CHUNK // 2
GROUP = CHUNK // DRAFT
HALO = 16
BACK = 4
RING = 6
MESH = pl.DeviceIdType.MESH
F32 = jnp.float32
BF16 = jnp.bfloat16
SERIES = (0.99999999, -0.49999941, 0.16665585, -0.04159356, 0.00810764, -0.00105947)


def lanes(b):
    return pl.ds(pl.multiple_of(b * BLOCK, BLOCK), BLOCK)


def rows_of(c, count):
    return pl.ds(pl.multiple_of(c * count, count), count)


def kernel(
    lag,
    n_req,
    n_ch,
    span_ref,
    accepted_ref,
    owner_ref,
    conv_ref,
    rate_ref,
    tokens_hbm,
    w_in_hbm,
    w_gate_hbm,
    gate_a_hbm,
    gate_i_hbm,
    w_out_hbm,
    state_hbm,
    cached_hbm,
    mout,
    ost,
    oin,
    w_cat,
    w_out,
    tok,
    gw,
    state,
    cached,
    cached_f,
    proj,
    inner,
    branch,
    hidden,
    kept,
    acc_b,
    inner_s,
    branch_s,
    local,
    decays,
    ends_a,
    ends_h,
    sum_send,
    sum_recv,
    own,
    stash_p,
    stash_q,
    send_p,
    send_q,
    recv_p,
    recv_q,
    send2_p,
    send2_q,
    recv2_p,
    recv2_q,
    gated_x,
    gated_r,
    pair_send,
    pair_recv,
    pair_own,
    last_send,
    last_recv,
    a2a_send,
    a2a_recv,
    rates,
    load_sem,
    w_sem,
    tok_sem,
    halo_send_sem,
    halo_recv_sem,
    sum_send_sem,
    sum_recv_sem,
    one_send,
    one_recv,
    two_send,
    two_recv,
    a2a_send_sem,
    a2a_recv_sem,
    piece_sem,
    spread_send,
    spread_recv,
    core_send,
    core_recv,
    pair_send_sem,
    pair_recv_sem,
):
    chans = w_in_hbm.shape[1]
    blocks = chans // BLOCK
    requests = accepted_ref.shape[1]
    slots = 2 * requests // n_req
    drafts = requests * DRAFT // CHUNK
    spans = SPAN_ROWS // CHUNK
    wides = 2 * chans // WIDE
    me = lax.axis_index("req")
    place = lax.axis_index("ch")
    odd = lax.rem(place, 2)
    mate = place + 1 - 2 * odd
    other = lax.rem(place + n_ch - 1 + 2 * odd, n_ch)
    far = lax.rem(place + 2, n_ch)
    mine = lax.rem((place + 1) // 2, 2)
    groups = n_req // n_ch
    piece_rows = chans // groups
    kind = me // groups
    piece = lax.rem(me, groups)

    def peer(j):
        return lax.rem(me + j, n_req)

    barrier = pltpu.get_barrier_semaphore()

    @pl.loop(1, n_req)
    def _(j):
        pl.semaphore_signal(barrier, inc=1, device_id={"req": peer(j)}, device_id_type=MESH)

    for side in (mate, other):
        pl.semaphore_signal(barrier, inc=1, device_id={"ch": side}, device_id_type=MESH)

    def load_weights(n):
        pieces = []
        for k, source in enumerate((w_in_hbm, w_gate_hbm)):
            low, high = max(n * WIDE, k * chans), min((n + 1) * WIDE, (k + 1) * chans)
            if low < high:
                pieces.append(
                    pltpu.make_async_copy(
                        source.at[:, pl.ds(low - k * chans, high - low)],
                        w_cat.at[:, pl.ds(low, high - low)],
                        w_sem.at[n, k],
                    )
                )
        return pieces

    small = [
        pltpu.make_async_copy(gate_a_hbm, gw.at[:, :, pl.ds(0, BLOCK)], load_sem.at[0]),
        pltpu.make_async_copy(gate_i_hbm, gw.at[:, :, pl.ds(BLOCK, BLOCK)], load_sem.at[1]),
        pltpu.make_async_copy(state_hbm, state, load_sem.at[2]),
        pltpu.make_async_copy(cached_hbm, cached, load_sem.at[3]),
    ]
    load_out = []
    for k, source in enumerate((far, other, place, mate)):
        columns = pl.ds(pl.multiple_of(source * chans, BLOCK), chans)
        load_out.append(
            pltpu.make_async_copy(
                w_out_hbm.at[:, columns], w_out.at[pl.ds(0, chans), pl.ds(k * chans, chans)], load_sem.at[4 + k]
            )
        )

    def load_tokens(i):
        return pltpu.make_async_copy(
            tokens_hbm.at[rows_of(i, CHUNK)],
            tok.at[pl.ds(pl.multiple_of(HALO + i * CHUNK, HALO), CHUNK)],
            tok_sem.at[i],
        )

    def token_rows(i):
        return tok[pl.ds(pl.multiple_of(HALO + i * CHUNK, HALO), CHUNK), :]

    load_tokens(spans).start()
    for n in range(wides):
        for copy in load_weights(n):
            copy.start()
    for copy in small:
        copy.start()

    def halo_copy():
        return pltpu.make_async_remote_copy(
            src_ref=tokens_hbm.at[pl.ds(SPAN_ROWS - HALO, HALO)],
            dst_ref=tok.at[pl.ds(0, HALO)],
            send_sem=halo_send_sem,
            recv_sem=halo_recv_sem,
            device_id={"req": peer(1)},
            device_id_type=MESH,
        )

    def first_copy(c, side):
        source, target, device = ((send_p, recv_p, mate), (send_q, recv_q, other))[side]
        return pltpu.make_async_remote_copy(
            src_ref=source.at[c],
            dst_ref=target.at[c],
            send_sem=one_send.at[c, side],
            recv_sem=one_recv.at[c, side],
            device_id={"ch": device},
            device_id_type=MESH,
        )

    def second_copy(c, side):
        source, target, device = ((send2_p, recv2_p, mate), (send2_q, recv2_q, other))[side]
        return pltpu.make_async_remote_copy(
            src_ref=source.at[c],
            dst_ref=target.at[c],
            send_sem=two_send.at[c, side],
            recv_sem=two_recv.at[c, side],
            device_id={"ch": device},
            device_id_type=MESH,
        )

    def a2a_copy(j):
        return pltpu.make_async_remote_copy(
            src_ref=a2a_send.at[peer(j)],
            dst_ref=a2a_recv.at[me],
            send_sem=a2a_send_sem.at[j],
            recv_sem=a2a_recv_sem.at[j],
            device_id={"req": peer(j)},
            device_id_type=MESH,
        )

    def sum_copy(j):
        return pltpu.make_async_remote_copy(
            src_ref=sum_send,
            dst_ref=sum_recv.at[j - 1],
            send_sem=sum_send_sem.at[j - 1],
            recv_sem=sum_recv_sem.at[j - 1],
            device_id={"req": peer(j)},
            device_id_type=MESH,
        )

    def spread_accepted():
        across = lax.broadcasted_iota(jnp.int32, (requests, requests), 1)
        down = lax.broadcasted_iota(jnp.int32, (requests, requests), 0)
        column = jnp.sum(
            jnp.where(across == down, accepted_ref[...], 0), axis=1, keepdims=True
        )
        acc_b[...] = jnp.broadcast_to(column, (requests, BLOCK))

    spread_accepted()

    firsts = [jnp.int32(0)]
    for i in range(span_ref.shape[0] - 1):
        firsts.append(firsts[-1] + span_ref[i])

    def project(tokens, n):
        at = slice(n * WIDE, (n + 1) * WIDE)
        proj[:, at] = jnp.dot(tokens, w_cat[:, at], preferred_element_type=F32)

    def gelu(u):
        return (0.5 * u) * (1.0 + jnp.tanh(u * (0.7978845608028654 + 0.035677408136300125 * (u * u))))

    def gates(conv, b):
        both = jnp.dot(conv.astype(BF16), gw[b], preferred_element_type=F32)
        rate_gate = 0.5 + 0.5 * jnp.tanh(0.5 * both[:, :BLOCK])
        input_gate = 0.5 + 0.5 * jnp.tanh(0.5 * both[:, BLOCK:])
        y = rates[0:1, lanes(b)] * rate_gate
        series = SERIES[-1]
        for term in SERIES[-2::-1]:
            series = series * y + term
        z = y * series
        drive = z * lax.rsqrt(jnp.maximum(z, 1e-37)) * input_gate * conv
        return jnp.exp(-0.5 * y), drive

    def spread():
        return jnp.concatenate([hidden[b] for b in range(blocks)], 1)

    def project_out(c, gated, opening=False):
        def shares(k):
            at = slice(k * chans, (k + 2) * chans)
            both = jnp.dot(gated, w_out[pl.ds(0, chans), at], preferred_element_type=F32)
            return both[:, :chans].astype(BF16), both[:, chans:].astype(BF16)

        to_far, to_other = shares(0)
        send_p[c, pl.ds(0, HALF)] = to_far[:HALF]
        send_q[c, pl.ds(0, HALF)] = to_far[HALF:]
        stash_q[c] = to_other[:HALF]
        send_q[c, pl.ds(HALF, HALF)] = to_other[HALF:]
        if opening:
            pl.semaphore_wait(barrier, n_req - 1 + 2)
            halo_copy().start()
            piece_copy().start()
        first_copy(c, 1).start()
        to_own, to_mate = shares(2)
        send_p[c, pl.ds(HALF, HALF)] = to_mate[:HALF]
        stash_p[c] = to_mate[HALF:]
        first_copy(c, 0).start()
        own[c] = to_own

    def pass_on(c):
        first_copy(c, 0).wait_recv()
        send2_q[c] = (recv_p[c, pl.ds(0, HALF)].astype(F32) + stash_q[c].astype(F32)).astype(BF16)
        second_copy(c, 1).start()
        first_copy(c, 1).wait_recv()
        send2_p[c] = (recv_q[c, pl.ds(0, HALF)].astype(F32) + stash_p[c].astype(F32)).astype(BF16)
        second_copy(c, 0).start()

    def slot_of_kind(device):
        step = lax.rem(kind - device + n_ch, n_ch)
        parity = lax.rem(device, 2)
        turned = lax.rem(step + parity * (n_ch - 2 * step) + n_ch, n_ch)
        return pl.multiple_of(lax.rem(turned + 2, n_ch) * chans, BLOCK)

    def piece_copy():
        rows = pl.multiple_of(piece * piece_rows, 16)
        columns = pl.multiple_of(kind * chans, BLOCK)
        return pltpu.make_async_remote_copy(
            src_ref=w_out_hbm.at[pl.ds(rows, piece_rows), pl.ds(columns, chans)],
            dst_ref=w_out.at[pl.ds(pl.multiple_of(chans + rows, 16), piece_rows), pl.ds(slot_of_kind(mate), chans)],
            send_sem=piece_sem.at[0],
            recv_sem=piece_sem.at[1],
            device_id={"ch": mate},
            device_id_type=MESH,
        )

    def spread_copy(j):
        rows = pl.multiple_of(chans + piece * piece_rows, 16)
        part = w_out.at[pl.ds(rows, piece_rows), pl.ds(slot_of_kind(place), chans)]
        return pltpu.make_async_remote_copy(
            src_ref=part,
            dst_ref=part,
            send_sem=spread_send.at[j],
            recv_sem=spread_recv.at[j],
            device_id={"req": peer(2 * j)},
            device_id_type=MESH,
        )

    def core_copy(g):
        rows = pl.multiple_of(chans + (2 * g + lax.rem(me, 2)) * piece_rows, 16)
        part = w_out.at[pl.ds(rows, piece_rows)]
        return pltpu.make_async_remote_copy(
            src_ref=part,
            dst_ref=part,
            send_sem=core_send.at[g],
            recv_sem=core_recv.at[g],
            device_id={"req": me + 1 - 2 * lax.rem(me, 2)},
            device_id_type=MESH,
        )

    def spread_pieces():
        piece_copy().wait_recv()

        @pl.loop(1, n_req // 2)
        def _(j):
            spread_copy(j).start()

    def swap_cores(g):
        for k in range(n_ch):
            source = k * groups + 2 * g + lax.rem(me, 2)
            j = lax.rem(me - source + n_req, n_req) // 2

            @pl.when(j > 0)
            def _():
                spread_copy(j).wait_recv()

        core_copy(g).start()

    def pair_copy(stage, j):
        source, target, device = (
            (gated_x.at[j, 1 - mine], gated_r.at[j], mate),
            (pair_send.at[0, j], pair_recv.at[0, j], other),
            (pair_send.at[1, j], pair_recv.at[1, j], other),
            (last_send.at[j], last_recv.at[j], mate),
        )[stage]
        return pltpu.make_async_remote_copy(
            src_ref=source,
            dst_ref=target,
            send_sem=pair_send_sem.at[stage, j],
            recv_sem=pair_recv_sem.at[stage, j],
            device_id={"ch": device},
            device_id_type=MESH,
        )

    def pair_project(j):
        pair_copy(0, j).wait_recv()
        both = jnp.concatenate([gated_x[j, mine], gated_r[j]], 1)
        outer = jnp.dot(both, w_out[:, : 2 * chans], preferred_element_type=F32)
        pair_send[0, j] = outer[:, :chans].astype(BF16)
        pair_copy(1, j).start()
        pair_send[1, j] = outer[:, chans:].astype(BF16)
        pair_copy(2, j).start()
        pair_own[j] = jnp.dot(both, w_out[:, 2 * chans :], preferred_element_type=F32)

    def pair_rows(j, chunk):
        first = RING + 2 * j
        base = jnp.where(first < drafts, SPAN_ROWS + first * CHUNK, (first - drafts) * CHUNK)
        return pl.ds(pl.multiple_of(base + chunk * CHUNK, CHUNK), CHUNK)

    def pair_sum(j):
        pair_copy(1, j).wait_recv()
        last_send[j] = (pair_own[j, :, chans:] + pair_recv[0, j].astype(F32)).astype(BF16)
        pair_copy(3, j).start()

    def pair_keep(j):
        pair_copy(2, j).wait_recv()
        total = pair_own[j, :, :chans] + pair_recv[1, j].astype(F32)
        mout[pair_rows(j, mine), :] = total.astype(BF16)

    def pair_finish(j):
        pair_copy(3, j).wait_recv()
        mout[pair_rows(j, 1 - mine), :] = last_recv[j]

    def finish(c):
        second_copy(c, 0).wait_recv()
        second_copy(c, 1).wait_recv()
        upper = own[c, pl.ds(0, HALF)].astype(F32) + recv2_q[c].astype(F32)
        lower = own[c, pl.ds(HALF, HALF)].astype(F32) + recv2_p[c].astype(F32)
        upper = upper + recv_p[c, pl.ds(HALF, HALF)].astype(F32)
        lower = lower + recv_q[c, pl.ds(HALF, HALF)].astype(F32)
        base = SPAN_ROWS + c * CHUNK
        mout[pl.ds(pl.multiple_of(base, HALF), HALF), :] = upper.astype(BF16)
        mout[pl.ds(pl.multiple_of(base + HALF, HALF), HALF), :] = lower.astype(BF16)

    step = lax.broadcasted_iota(jnp.int32, (CHUNK, BLOCK), 0)
    offset = (step % GROUP) * DRAFT + step // GROUP

    def edge_rows():
        halo_copy().wait_recv()
        edge = tok[pl.ds(0, HALO), :]
        for b in range(blocks):
            columns = w_cat[:, b * BLOCK : (b + 1) * BLOCK]
            inner_s[b, pl.ds(0, HALO)] = (
                jnp.dot(edge, columns, preferred_element_type=F32).astype(BF16).astype(F32)
            )

    def span_chunk(q, following):
        for b in range(blocks):
            inner_s[b, pl.ds(pl.multiple_of(HALO + q * CHUNK, HALO), CHUNK)] = (
                proj[:, b * BLOCK : (b + 1) * BLOCK].astype(BF16).astype(F32)
            )
        branch_s[rows_of(q, CHUNK), :] = gelu(proj[:, chans:])
        position = me * SPAN_ROWS + q * CHUNK + offset
        begin = jnp.zeros((CHUNK, BLOCK), jnp.int32)
        for first in firsts:
            begin = jnp.where(first <= position, first, begin)
        age = position - begin
        tokens = token_rows(following)
        base = HALO - HIST + q * CHUNK
        for b in range(blocks):
            project(tokens, b)
            rows = [
                inner_s[b, pl.ds(base + i, GROUP, stride=DRAFT), :] for i in range(DRAFT + HIST)
            ]
            x = jnp.concatenate(rows, 0)
            conv = conv_ref[0:1, lanes(b)] * x[HIST * GROUP : HIST * GROUP + CHUNK]
            for k in range(1, CONV):
                at = (HIST - k) * GROUP
                term = conv_ref[k : k + 1, lanes(b)] * x[at : at + CHUNK]
                conv = conv + jnp.where(age >= k, term, 0.0)
            decay, drive = gates(conv, b)
            decay = jnp.where(age > 0, decay, 0.0)
            h = jnp.zeros((GROUP, BLOCK), F32)
            a = jnp.ones((GROUP, BLOCK), F32)
            for t in range(DRAFT):
                part = slice(t * GROUP, (t + 1) * GROUP)
                h = decay[part] * h + drive[part]
                a = decay[part] * a
                at = pl.ds(pl.multiple_of(q * CHUNK + t * GROUP, GROUP), GROUP)
                local[at, lanes(b)] = h
                decays[at, lanes(b)] = a
            ends_a[rows_of(q, GROUP), lanes(b)] = a
            ends_h[rows_of(q, GROUP), lanes(b)] = h

    def link(s, carry):
        product, value = carry
        at = pl.ds(s, 1)
        a = ends_a[at, :]
        h = ends_h[at, :]
        ends_a[at, :] = product
        ends_h[at, :] = value
        return (a * product, a * value + h)

    def send_sums():
        product, value = lax.fori_loop(
            0, spans * GROUP, link, (jnp.ones((1, chans), F32), jnp.zeros((1, chans), F32))
        )
        sum_send[...] = jnp.zeros_like(sum_send)
        sum_send[0:1, :] = product
        sum_send[1:2, :] = value
        for j in range(1, BACK + 1):
            sum_copy(j).start()

    def draft_chunk(c, following):
        for b in range(blocks):
            inner[b] = proj[:, b * BLOCK : (b + 1) * BLOCK].astype(BF16).astype(F32)
        branch[...] = gelu(proj[:, chans:])
        members = rows_of(c, GROUP)
        accepted = acc_b[members, :]
        chosen = [accepted == t + 1 for t in range(DRAFT)]
        tokens = token_rows(following)
        for b in range(blocks):
            project(tokens, b)
            rows = [cached_f[j, members, lanes(b)] for j in range(HIST)]
            rows += [inner[b, pl.ds(t, GROUP, stride=DRAFT), :] for t in range(DRAFT)]
            x = jnp.concatenate(rows, 0)
            conv = 0.0
            for k in range(CONV):
                at = (HIST - k) * GROUP
                conv = conv + conv_ref[k : k + 1, lanes(b)] * x[at : at + CHUNK]
            decay, drive = gates(conv, b)
            h = state[members, lanes(b)]
            picked = [jnp.zeros((GROUP, BLOCK), F32) for _ in range(1 + HIST)]
            for t in range(DRAFT):
                part = slice(t * GROUP, (t + 1) * GROUP)
                h = decay[part] * h + drive[part]
                hidden[b, pl.ds(t, GROUP, stride=DRAFT), :] = h
                picked[0] = jnp.where(chosen[t], h, picked[0])
                for j in range(HIST):
                    picked[1 + j] = jnp.where(chosen[t], rows[t + 1 + j], picked[1 + j])
            for j in range(1 + HIST):
                at = pl.ds(pl.multiple_of(j * requests + c * GROUP, GROUP), GROUP)
                kept[at, lanes(b)] = picked[j]
        return (branch[...] * spread()).astype(BF16)

    load_tokens(spans).wait()
    tokens = token_rows(spans)
    for n in range(wides):
        for copy in load_weights(n):
            copy.wait()
        project(tokens, n)

    for copy in load_out:
        copy.start()
    for q in range(spans):
        load_tokens(q).start()

    @pl.loop(spans + 1, spans + drafts)
    def _(i):
        load_tokens(i).start()

    for copy in small:
        copy.wait()
    cached_f[...] = cached[...].astype(F32)
    rates[0:1, :] = 16.0 * rate_ref[...].reshape(1, chans)
    for copy in load_out:
        copy.wait()
    load_tokens(spans + 1).wait()
    project_out(0, draft_chunk(0, spans + 1), opening=True)

    @pl.loop(0, spans)
    def _(i):
        load_tokens(i).wait()
        project_out(i + 1, draft_chunk(i + 1, i))

        @pl.when(i == 0)
        def _():
            edge_rows()
            spread_pieces()

        @pl.when(i > 0)
        def _():
            pass_on(i - 1)

        load_tokens(spans + 2 + i).wait()
        span_chunk(i, spans + 2 + i)

    send_sums()

    def draft_step(c):
        @pl.when(c < drafts - 1)
        def _():
            load_tokens(spans + 1 + c).wait()

        return draft_chunk(c, spans + jnp.minimum(c + 1, drafts - 1))

    @pl.loop(spans + 1, RING)
    def _(c):
        project_out(c, draft_step(c))
        pass_on(c - lag)

    for j in range(1, BACK + 1):
        sum_copy(j).wait_recv()
    entering = sum_recv[BACK - 1, 1:2, :]
    for j in range(BACK - 2, -1, -1):
        entering = sum_recv[j, 0:1, :] * entering + sum_recv[j, 1:2, :]

    @pl.loop(0, spans)
    def _(q):
        carry = ends_h[rows_of(q, GROUP), :] + ends_a[rows_of(q, GROUP), :] * entering
        for t in range(DRAFT):
            at = pl.ds(pl.multiple_of(q * CHUNK + t * GROUP, GROUP), GROUP)
            h = local[at, :] + decays[at, :] * carry
            for b in range(blocks):
                hidden[b, pl.ds(t, GROUP, stride=DRAFT), :] = h[:, b * BLOCK : (b + 1) * BLOCK]
        gated_x[1 + q // 2, lax.rem(q, 2)] = (branch_s[rows_of(q, CHUNK), :] * spread()).astype(BF16)

        @pl.when(lax.rem(q, 2) == 1)
        def _():
            pair_copy(0, 1 + q // 2).start()

    for g in range(groups // 2):
        swap_cores(g)

    @pl.loop(RING, drafts)
    def _(c):
        gated_x[0, c - RING] = draft_step(c)
        pass_on(c - lag)

    pair_copy(0, 0).start()

    for g in range(groups // 2):
        core_copy(g).wait_recv()
    pairs = (drafts + spans - RING) // 2

    @pl.loop(0, pairs)
    def _(j):
        pair_project(lax.rem(j + 1, pairs))

    owner_row = owner_ref[...]
    across = lax.broadcasted_iota(jnp.int32, (requests, requests), 1)
    down = lax.broadcasted_iota(jnp.int32, (requests, requests), 0)
    owner_column = jnp.sum(jnp.where(across == down, owner_row, 0), axis=1, keepdims=True)
    same = jnp.where(owner_column == owner_row, 1, 0)
    rank_row = jnp.sum(jnp.where(down < across, same, 0), axis=0, keepdims=True)
    slot_row = owner_row * slots + rank_row
    kinds = 1 + HIST
    tall = n_req * kinds * slots
    item = lax.broadcasted_iota(jnp.int32, (tall, requests), 0)
    slot_of = (item // (kinds * slots)) * slots + item % slots
    kind_of = (item // slots) % kinds
    hit = jnp.where(slot_of == slot_row, 1.0, 0.0)
    total = jnp.zeros((tall, chans), F32)
    for j in range(kinds):
        pick = jnp.where(kind_of == j, hit, 0.0).astype(BF16)
        total = total + jnp.dot(
            pick,
            kept[pl.ds(j * requests, requests), :].astype(BF16),
            preferred_element_type=F32,
        )
    a2a_send[...] = total.astype(BF16).reshape(n_req, kinds * slots, chans)

    @pl.loop(1, n_req)
    def _(j):
        a2a_copy(j).start()

    local_copy = pltpu.make_async_copy(a2a_send.at[me], a2a_recv.at[me], a2a_send_sem.at[0])
    local_copy.start()

    pair_sum(1)
    pair_keep(1)
    pair_sum(2)

    @pl.loop(0, RING)
    def _(c):
        finish(c)

    pair_keep(2)
    pair_sum(0)

    local_copy.wait()

    @pl.loop(1, n_req)
    def _(j):
        a2a_copy(j).wait_recv()

    got = a2a_recv[...]
    ost[...] = got[:, :slots].astype(F32).reshape(n_req * slots, chans)
    for j in range(HIST):
        oin[j] = (
            got[:, (1 + j) * slots : (2 + j) * slots].astype(F32).reshape(n_req * slots, chans).astype(BF16)
        )
    pair_keep(0)
    for j in (1, 2, 0):
        pair_finish(j)

    halo_copy().wait_send()
    piece_copy().wait_send()

    @pl.loop(1, n_req // 2)
    def _(j):
        spread_copy(j).wait_send()

    for g in range(groups // 2):
        core_copy(g).wait_send()

    @pl.loop(0, pairs)
    def _(j):
        for stage in range(4):
            pair_copy(stage, j).wait_send()

    for j in range(1, BACK + 1):
        sum_copy(j).wait_send()

    @pl.loop(1, n_req)
    def _(j):
        a2a_copy(j).wait_send()

    @pl.loop(0, RING)
    def _(c):
        for side in range(2):
            first_copy(c, side).wait_send()
            second_copy(c, side).wait_send()


def write_out(*refs):
    sources, targets, sems = refs[:3], refs[3:6], refs[6]
    copies = [
        pltpu.make_async_copy(source, target, sems.at[i])
        for i, (source, target) in enumerate(zip(sources, targets))
    ]
    for copy in copies:
        copy.start()
    for copy in copies:
        copy.wait()


def per_device(
    n_req,
    n_ch,
    tokens,
    w_in,
    w_gate,
    gate_a,
    gate_i,
    conv_w,
    decay_rate,
    w_out,
    cached_state,
    cached_inputs,
    span_lengths,
    accepted,
    owner,
):
    rows, width = tokens.shape
    chans = w_in.shape[1]
    blocks = chans // BLOCK
    requests = accepted.shape[0]
    slots = 2 * requests // n_req
    kinds = 1 + HIST
    drafts = requests * DRAFT // CHUNK
    spans = SPAN_ROWS // CHUNK
    chunks = drafts + spans
    pairs = (chunks - RING) // 2
    lag = min(2, spans)
    vmem, anywhere, smem = (
        pl.BlockSpec(memory_space=pltpu.VMEM),
        pl.BlockSpec(memory_space=pl.ANY),
        pl.BlockSpec(memory_space=pltpu.SMEM),
    )
    dma = pltpu.SemaphoreType.DMA
    mixed, ostate, oin = pl.pallas_call(
        functools.partial(kernel, lag, n_req, n_ch),
        out_shape=(
            pltpu.VMEM((rows, chans), BF16),
            pltpu.VMEM((n_req * slots, chans), F32),
            pltpu.VMEM((HIST, n_req * slots, chans), BF16),
        ),
        in_specs=[smem, vmem, vmem, vmem, vmem] + [anywhere] * 8,
        out_specs=(vmem, vmem, vmem),
        scratch_shapes=[
            pltpu.VMEM((width, 2 * chans), BF16),
            pltpu.VMEM((2 * chans, n_ch * chans), BF16),
            pltpu.VMEM((HALO + rows, width), BF16),
            pltpu.VMEM((blocks, BLOCK, 2 * BLOCK), BF16),
            pltpu.VMEM((requests, chans), F32),
            pltpu.VMEM((HIST, requests, chans), BF16),
            pltpu.VMEM((HIST, requests, chans), F32),
            pltpu.VMEM((CHUNK, 2 * chans), F32),
            pltpu.VMEM((blocks, CHUNK, BLOCK), F32),
            pltpu.VMEM((CHUNK, chans), F32),
            pltpu.VMEM((blocks, CHUNK, BLOCK), F32),
            pltpu.VMEM((kinds * requests, chans), F32),
            pltpu.VMEM((requests, BLOCK), jnp.int32),
            pltpu.VMEM((blocks, HALO + SPAN_ROWS, BLOCK), F32),
            pltpu.VMEM((SPAN_ROWS, chans), F32),
            pltpu.VMEM((SPAN_ROWS, chans), F32),
            pltpu.VMEM((SPAN_ROWS, chans), F32),
            pltpu.VMEM((spans * GROUP, chans), F32),
            pltpu.VMEM((spans * GROUP, chans), F32),
            pltpu.VMEM((8, chans), F32),
            pltpu.VMEM((BACK, 8, chans), F32),
            pltpu.VMEM((RING, CHUNK, chans), BF16),
            pltpu.VMEM((RING, HALF, chans), BF16),
            pltpu.VMEM((RING, HALF, chans), BF16),
            pltpu.VMEM((RING, CHUNK, chans), BF16),
            pltpu.VMEM((RING, CHUNK, chans), BF16),
            pltpu.VMEM((RING, CHUNK, chans), BF16),
            pltpu.VMEM((RING, CHUNK, chans), BF16),
            pltpu.VMEM((RING, HALF, chans), BF16),
            pltpu.VMEM((RING, HALF, chans), BF16),
            pltpu.VMEM((RING, HALF, chans), BF16),
            pltpu.VMEM((RING, HALF, chans), BF16),
            pltpu.VMEM((pairs, 2, CHUNK, chans), BF16),
            pltpu.VMEM((pairs, CHUNK, chans), BF16),
            pltpu.VMEM((2, pairs, CHUNK, chans), BF16),
            pltpu.VMEM((2, pairs, CHUNK, chans), BF16),
            pltpu.VMEM((pairs, CHUNK, 2 * chans), F32),
            pltpu.VMEM((pairs, CHUNK, chans), BF16),
            pltpu.VMEM((pairs, CHUNK, chans), BF16),
            pltpu.VMEM((n_req, kinds * slots, chans), BF16),
            pltpu.VMEM((n_req, kinds * slots, chans), BF16),
            pltpu.VMEM((8, chans), F32),
            dma((9,)),
            dma((2 * chans // WIDE, 2)),
            dma((chunks,)),
            dma,
            dma,
            dma((BACK,)),
            dma((BACK,)),
            dma((RING, 2)),
            dma((RING, 2)),
            dma((RING, 2)),
            dma((RING, 2)),
            dma((n_req,)),
            dma((n_req,)),
            dma((2,)),
            dma((n_req // 2,)),
            dma((n_req // 2,)),
            dma((n_req // n_ch // 2,)),
            dma((n_req // n_ch // 2,)),
            dma((4, pairs)),
            dma((4, pairs)),
        ],
        compiler_params=pltpu.CompilerParams(
            collective_id=0, has_side_effects=True, vmem_limit_bytes=52 * 1024 * 1024
        ),
        name="griffin",
    )(
        span_lengths,
        accepted.reshape(1, requests),
        owner.reshape(1, requests),
        conv_w,
        decay_rate,
        tokens,
        w_in,
        w_gate,
        gate_a,
        gate_i,
        w_out,
        cached_state,
        jnp.transpose(cached_inputs, (1, 0, 2)),
    )
    mixed, ostate, oin = pl.pallas_call(
        write_out,
        out_shape=tuple(jax.ShapeDtypeStruct(a.shape, a.dtype) for a in (mixed, ostate, oin)),
        in_specs=[vmem] * 3,
        out_specs=(anywhere,) * 3,
        scratch_shapes=[dma((3,))],
        name="write_out",
    )(*(pltpu.with_memory_space_constraint(a, pltpu.VMEM) for a in (mixed, ostate, oin)))
    return (
        mixed,
        ostate.reshape(1, n_req * slots, chans),
        jnp.transpose(oin, (1, 0, 2)).reshape(1, n_req * slots, HIST, chans),
    )


def solution(mesh):
    return jax.shard_map(
        functools.partial(per_device, mesh.shape["req"], mesh.shape["ch"]),
        mesh=mesh,
        in_specs=(
            P("req", None),
            P(None, "ch"),
            P(None, "ch"),
            P("ch", None, None),
            P("ch", None, None),
            P(None, "ch"),
            P("ch"),
            P("ch", None),
            P("req", "ch"),
            P("req", None, "ch"),
            P(),
            P("req"),
            P("req", None),
        ),
        out_specs=(P("req", "ch"), P("req", None, "ch"), P("req", None, None, "ch")),
        check_vma=False,
    )
```
